32 devices in a mesh: dp: 8 (over y, x, core), expert: 4 (over z).
Axes of the slice: x: 2, y: 2, z: 4, core: 2. Of those that a mesh axis runs over, the one named last changes fastest.
Arguments:
- tokens: bfloat16 [256, 2048], P(('dp', 'expert')), may hold values from -6 to 6
- cotangent: bfloat16 [256, 2048], P(('dp', 'expert')), may hold values from -6 to 6
- expert_picks: int32 [256, 2], P(('dp', 'expert')), may hold values from 0 to 3, all different within a row; in each aligned block of 8 rows (0 to 7, 8 to 15, ...) at most 8 rows name the same one
- w_gate: bfloat16 [4, 2048, 8192], P('expert', None, 'dp'), may hold values from -0.125 to 0.125
- w_up: bfloat16 [4, 2048, 8192], P('expert', None, 'dp'), may hold values from -0.125 to 0.125
- w_down: bfloat16 [4, 8192, 2048], P('expert', 'dp'), may hold values from -0.0625 to 0.0625
- router: float32 [4, 2048], replicated, may hold values from -0.125 to 0.125
- norm_gain: float32 [2048], replicated, may hold values from 0.1 to 1.9
Outputs:
- token_grad: bfloat16 [256, 2048], P(('dp', 'expert'))
- router_grad: float32 [4, 2048], replicated
- gain_grad: float32 [2048], replicated
The draws below stay inside these ranges and needn't reach their ends.
Inputs may be any that keep to these rules, and one draw needn't show every extreme that they name: `expert_picks`: in each aligned block of 8 rows (the rows of one device) the two picks of a row differ, no expert is named by more than 8 rows, a bound that some block reaches.
All inputs are finite; a program needn't handle non-finite values.
Results may differ from the reference program's by a relative error of at most 0.015.
Values may be sent and summed in bfloat16 or wider, within the bound.
A program may use at most 64 MiB of HBM per device.

```python
import math
import jax
import jax.numpy as jnp
import numpy as np
from jax import lax

D = 2048
FF = 8192
T_DEV = 8
FF_DEV = 1024
E = 4
CAP = 8
TOKENS = 256
N_DP = 8


def block_levels(stream_key, shape, shards, smallest, largest):
    gain, own = 1.0, jax.random.fold_in(stream_key, 6)
    for position, shards_of in shards:
        draws = jnp.exp(jax.random.uniform(jax.random.fold_in(own, position), (shards_of,), jnp.float32, smallest / len(shards), largest / len(shards)))
        gain = gain * jnp.repeat(draws, shape[position] // shards_of).reshape([-1 if axis == position else 1 for axis in range(len(shape))])
    return gain


def deal_out(rng, own, number, rows, amount, top, bound, lean):
    order = jax.random.permutation(rng, amount)
    packed, ordinary = portions_of(amount, rows * top, bound, lean, True), portions_of(amount, rows * top, bound, lean, False)
    places = jnp.arange(amount)

    def named(tallies, offset_by):
        used = int((tallies > 0).sum())
        fixed = max(1, used // 4)
        passed = fixed + (places - fixed + offset_by * (used - fixed)) % max(1, amount - fixed)
        return jnp.zeros((amount,), jnp.int32).at[order[jnp.where(places < fixed, places, passed)]].set(jnp.asarray(tallies, jnp.int32))

    tallies = jnp.where(number % 4 == 0, named(packed, number // 4), named(ordinary, number - number // 4 - 1))
    mixed = jax.random.permutation(jax.random.fold_in(own, 3), amount)
    donor, taker = mixed[0:amount // 2 * 2:2], mixed[1:amount // 2 * 2:2]
    room = jnp.minimum(tallies[donor] - 1, bound - tallies[taker]) // 2
    room = jnp.where((donor == order[0]) | (taker == order[0]) | (tallies[taker] == 0), 0, jnp.maximum(room, 0))
    passed = jax.random.randint(jax.random.fold_in(own, 4), (amount // 2,), 0, 1 << 20) % (room + 1)
    tallies = tallies.at[donor].add(-passed).at[taker].add(passed)
    items = jnp.searchsorted(jnp.cumsum(tallies), jnp.arange(rows * top), side="right").astype(jnp.int32)
    listing = items.reshape(top, rows).T
    listing = listing[jax.random.permutation(jax.random.fold_in(own, 1), rows)]
    offset_by = jax.random.randint(jax.random.fold_in(own, 2), (rows, 1), 0, top)
    return jnp.take_along_axis(listing, (jnp.arange(top)[None, :] + offset_by) % top, axis=1)


def portions_of(number_of, total, reach, lean, full):
    portions = [(1 << 20) // math.isqrt(grade ** lean) + 1 for grade in range(1, number_of + 1)]
    largest = reach if full else min(reach, max(-(-total // number_of), total * portions[0] // sum(portions)))
    least = 1 if total - largest >= number_of - 1 else 0
    holding, rest = [largest] + [least] * (number_of - 1), total - largest - least * (number_of - 1)
    while rest > 0:
        candidates = [i for i in range(1, number_of) if holding[i] < largest] or [i for i in range(1, number_of) if holding[i] < reach]
        pool, left = sum([portions[i] for i in candidates]), rest
        for i in candidates:
            more = min(reach - holding[i], max(1, left * portions[i] // pool), rest)
            holding[i] = holding[i] + more
            rest = rest - more
    return np.array(holding)


def normal_values(own_key, dims, scale, reach, pieces=(), kind=jnp.bfloat16):
    entries = scale * jax.random.normal(own_key, dims, jnp.float32)
    if pieces:
        entries = entries * block_levels(own_key, dims, pieces, -0.22, 0.18)
    return jnp.clip(entries, -reach, reach).astype(kind)


def setup_inputs(seed: int = 0) -> dict:
    arg_keys = jax.random.split(jax.random.key(seed), 9)
    tokens = normal_values(arg_keys[0], (TOKENS, D), 1.0, 6.0, ((0, 32),))
    cotangent = normal_values(arg_keys[1], (TOKENS, D), 1.0, 6.0, ((0, 32),))
    expert_picks_keys = jax.random.split(jax.random.fold_in(arg_keys[2], 1), TOKENS // T_DEV)
    expert_picks_turns = jax.random.permutation(jax.random.fold_in(arg_keys[2], 3), TOKENS // T_DEV)
    expert_picks = jax.vmap(lambda own, number: deal_out(jax.random.fold_in(arg_keys[2], 2), own, number, T_DEV, E, 2, CAP, 2))(expert_picks_keys, expert_picks_turns).reshape((TOKENS, 2))
    w_gate = normal_values(arg_keys[3], (E, D, FF), D ** -0.5, 0.125, ((0, 4), (2, 8)))
    w_up = normal_values(arg_keys[4], (E, D, FF), D ** -0.5, 0.125, ((0, 4), (2, 8)))
    w_down = normal_values(arg_keys[5], (E, FF, D), FF ** -0.5, 0.0625, ((0, 4), (1, 8)))
    router = normal_values(arg_keys[6], (E, D), D ** -0.5, 0.125, (), jnp.float32)
    norm_gain = jnp.clip(1.0 + 0.18 * jax.random.normal(arg_keys[7], (D,), jnp.float32), 0.1, 1.9)
    return dict(tokens=tokens, cotangent=cotangent, expert_picks=expert_picks, w_gate=w_gate, w_up=w_up, w_down=w_down, router=router, norm_gain=norm_gain)


EPSILON = 1e-05
highest_precision = lax.Precision.HIGHEST

def silu_grad(pre_act):
    sigmoid_value = jax.nn.sigmoid(pre_act)
    return sigmoid_value + pre_act * sigmoid_value * (1.0 - sigmoid_value)

def reference(tokens, cotangent, expert_picks, w_gate, w_up, w_down, router, norm_gain):
    x_float = tokens.astype(jnp.float32)
    inverse = 1.0 / jnp.sqrt(lax.optimization_barrier(jnp.mean(x_float * x_float, axis=-1, keepdims=True)) + EPSILON)
    normed = x_float * inverse
    hidden = (normed * norm_gain).astype(jnp.bfloat16)
    logits = jnp.dot(hidden.astype(jnp.float32), router.T, precision=highest_precision)
    expert_ids = jnp.arange(E, dtype=jnp.int32)
    first_hot = (expert_picks[:, 0:1] == expert_ids).astype(jnp.float32)
    second_hot = (expert_picks[:, 1:2] == expert_ids).astype(jnp.float32)
    gate_first = jax.nn.sigmoid(lax.optimization_barrier(jnp.sum(logits * first_hot, -1)) - lax.optimization_barrier(jnp.sum(logits * second_hot, -1)))
    gate_second = 1.0 - gate_first
    gate_flat = jnp.stack([gate_first, gate_second], axis=1).reshape(-1)
    pair_expert = expert_picks.reshape(-1).astype(jnp.int32)
    blocks = pair_expert.reshape(-1, 2 * T_DEV)
    block_hot = (blocks[:, :, None] == expert_ids).astype(jnp.int32)
    slot_rank = (lax.optimization_barrier(jnp.sum(jnp.cumsum(block_hot, axis=1) * block_hot, axis=2)) - 1).reshape(-1).astype(jnp.int32)
    pair_ids = jnp.arange(2 * TOKENS, dtype=jnp.int32)
    block_of = (pair_ids // (2 * T_DEV)).astype(jnp.int32)
    slot_table = jnp.full((E, TOKENS // T_DEV, CAP), -1, jnp.int32).at[pair_expert, block_of, slot_rank].set(pair_ids)

    def per_expert(running, stacked):
        hidden_sum, inner_all = running
        gate_matrix, up_matrix, down_matrix, slot_index = stacked
        slot_index = slot_index.reshape(-1)
        is_valid = slot_index >= 0
        pair_index = jnp.maximum(slot_index, 0)
        token_index = pair_index // 2
        valid_bf = is_valid[:, None].astype(jnp.bfloat16)
        valid_float = is_valid.astype(jnp.float32)
        slot_rows = hidden[token_index] * valid_bf
        slot_cots = cotangent[token_index] * valid_bf
        pre_gate = jnp.dot(slot_rows, gate_matrix, preferred_element_type=jnp.float32)
        pre_up = jnp.dot(slot_rows, up_matrix, preferred_element_type=jnp.float32)
        act = (jax.nn.silu(pre_gate) * pre_up).astype(jnp.bfloat16)
        cot_back = lax.dot_general(slot_cots, down_matrix, (((1,), (1,)), ((), ())), preferred_element_type=jnp.float32)
        pick_inner = lax.optimization_barrier(jnp.sum(act.astype(jnp.float32) * cot_back, -1)) * valid_float
        d_gate = (cot_back * pre_up * silu_grad(pre_gate)).astype(jnp.bfloat16)
        d_up = (cot_back * jax.nn.silu(pre_gate)).astype(jnp.bfloat16)

        def add_group(group, total):
            first = (group * FF_DEV).astype(jnp.int32)
            gate_part = lax.dynamic_slice_in_dim(d_gate, first, FF_DEV, 1)
            up_part = lax.dynamic_slice_in_dim(d_up, first, FF_DEV, 1)
            gate_cols = lax.dynamic_slice_in_dim(gate_matrix, first, FF_DEV, 1)
            up_cols = lax.dynamic_slice_in_dim(up_matrix, first, FF_DEV, 1)
            part = lax.dot_general(gate_part, gate_cols, (((1,), (1,)), ((), ())), preferred_element_type=jnp.float32)
            part = part + lax.dot_general(up_part, up_cols, (((1,), (1,)), ((), ())), preferred_element_type=jnp.float32)
            rounded = lax.optimization_barrier(part.astype(jnp.bfloat16))
            return total + rounded.astype(jnp.float32)
        summed = lax.fori_loop(0, N_DP, add_group, jnp.zeros((slot_rows.shape[0], D), jnp.float32))
        pair_grad = lax.optimization_barrier(summed.astype(jnp.bfloat16)).astype(jnp.float32)
        weight = (gate_flat[pair_index] * valid_float)[:, None]
        inner_all = inner_all.at[pair_index].add(pick_inner)
        hidden_sum = hidden_sum.at[token_index].add(pair_grad * weight)
        return ((hidden_sum, inner_all), None)
    start = (jnp.zeros((TOKENS, D), jnp.float32), jnp.zeros((2 * TOKENS,), jnp.float32))
    (hidden_sum, inner_all), unused = lax.scan(per_expert, start, (w_gate, w_up, w_down, slot_table))
    pick_inner = inner_all.reshape(TOKENS, 2)
    gate_delta = gate_first * gate_second * (pick_inner[:, 0] - pick_inner[:, 1])
    logit_grad = (first_hot - second_hot) * gate_delta[:, None]
    hidden_grad = hidden_sum + jnp.dot(logit_grad, router, precision=highest_precision)
    router_grad = jnp.dot(logit_grad.T, hidden.astype(jnp.float32), precision=highest_precision)
    gain_grad = lax.optimization_barrier(jnp.sum(hidden_grad * normed, axis=0))
    scaled_grad = hidden_grad * norm_gain
    token_grad = cotangent.astype(jnp.float32) + inverse * (scaled_grad - normed * lax.optimization_barrier(jnp.mean(scaled_grad * normed, axis=-1, keepdims=True)))
    return (token_grad.astype(jnp.bfloat16), router_grad, gain_grad)
```

```python
import functools

import jax
import jax.numpy as jnp
from jax import lax
from jax.experimental import pallas as pl
from jax.experimental.pallas import tpu as pltpu
from jax.sharding import PartitionSpec as P

EPSILON = 1e-05
highest_precision = lax.Precision.HIGHEST


def silu_grad(pre_act):
    sigmoid_value = jax.nn.sigmoid(pre_act)
    return sigmoid_value + pre_act * sigmoid_value * (1.0 - sigmoid_value)


def expert_pass(slot_rows, slot_cots, gate_shard, up_shard, down_shard):
    pre_gate = jnp.dot(slot_rows, gate_shard, preferred_element_type=jnp.float32)
    pre_up = jnp.dot(slot_rows, up_shard, preferred_element_type=jnp.float32)
    act = (jax.nn.silu(pre_gate) * pre_up).astype(jnp.bfloat16)
    cot_back = lax.dot_general(
        slot_cots, down_shard, (((1,), (1,)), ((), ())), preferred_element_type=jnp.float32
    )
    pick_part = jnp.sum(act.astype(jnp.float32) * cot_back, -1)
    d_gate = (cot_back * pre_up * silu_grad(pre_gate)).astype(jnp.bfloat16)
    d_up = (cot_back * jax.nn.silu(pre_gate)).astype(jnp.bfloat16)
    d_rows = lax.dot_general(
        d_gate, gate_shard, (((1,), (1,)), ((), ())), preferred_element_type=jnp.float32
    )
    d_rows = d_rows + lax.dot_general(
        d_up, up_shard, (((1,), (1,)), ((), ())), preferred_element_type=jnp.float32
    )
    return (d_rows, pick_part)


NT = (((1,), (1,)), ((), ()))
F32 = jnp.float32
BF16 = jnp.bfloat16


def split3(v):
    hi = v.astype(BF16).astype(F32)
    mid = (v - hi).astype(BF16).astype(F32)
    return hi, mid, v - hi - mid


def store_split(ref, v):
    n = v.shape[0]
    ref[...] = jnp.zeros_like(ref)
    for i, part in enumerate(split3(v)):
        ref[8 * i : 8 * i + n, :] = part


def join_split(v, n):
    return v[0:n] + v[8 : 8 + n] + v[16 : 16 + n]


def dense_kernel(
    experts, tok_ref, cot_ref, picks_ref, wg_hbm, wu_hbm, wd_hbm, router_ref, gain_ref,
    out_tok, out_router, out_gain,
    buf, wg, wu, wd, hid, tok, cot, norm, inv, dg, du, wcol, lgcol, rsp, lsp, lspi,
    pbuf, cbuf, sbuf, plbuf, zsrc, zbuf, pickcol, vsrc, cvec, vchip, pvec, vplane, zvec,
    lsem, wsem, agr, zs, xs, ys, cs, dxs, dys, rs_s, rs_r, pl_s, pl_r, zz_s, zz_r, vs, vr,
):
    width = tok_ref.shape[1]
    tok_count = tok_ref.shape[0]
    blocks = buf.shape[0]
    total = blocks * tok_count
    ff = wg.shape[1]
    dp = lax.axis_index("dp")
    ex = lax.axis_index("expert")
    core = lax.rem(dp, 2)
    group = lax.div(dp, 2)
    xbit = lax.rem(group, 2)
    ybit = lax.div(group, 2)
    to_core = 1 - 2 * core
    to_x = 1 - 2 * xbit
    to_y = 2 * (1 - 2 * ybit)
    dp_c = dp + to_core
    dp_x = dp + 2 * to_x
    dp_y = dp + 2 * to_y
    dp_d = dp + 2 * (to_x + to_y)
    me = dp * experts + ex

    tile = ff // 4
    wcopies = []
    for t in range(4):
        part = pl.ds(t * tile, tile)
        three = (
            pltpu.make_async_copy(wg_hbm.at[0, :, part], wg.at[:, part], wsem.at[3 * t]),
            pltpu.make_async_copy(wu_hbm.at[0, :, part], wu.at[:, part], wsem.at[3 * t + 1]),
            pltpu.make_async_copy(wd_hbm.at[0, part, :], wd.at[part, :], wsem.at[3 * t + 2]),
        )
        wcopies.append(three)
    load_t = pltpu.make_async_copy(tok_ref, buf.at[me, 0, :, pl.ds(0, width)], lsem.at[0])
    load_c = pltpu.make_async_copy(cot_ref, buf.at[me, 1, :, pl.ds(0, width)], lsem.at[1])
    load_t.start()
    load_c.start()
    picks = picks_ref[...].astype(F32)
    lane = lax.broadcasted_iota(jnp.int32, (tok_count, 128), 1)
    picks_tile = jnp.where(lane == 0, picks[:, 0:1], jnp.where(lane == 1, picks[:, 1:2], 0.0))
    buf[me, 0, :, width : width + 128] = picks_tile.astype(BF16)
    buf[me, 1, :, width : width + 128] = jnp.zeros((tok_count, 128), BF16)
    for three in wcopies:
        for cp in three:
            cp.start()

    def where_is(d, z):
        return {"dp": d, "expert": z}

    barrier = pltpu.get_barrier_semaphore()
    peers = [(dp_c, ex), (dp_x, ex), (dp_y, ex), (dp_d, ex)]
    peers += [(dp, lax.rem(ex + k, experts)) for k in range(1, experts)]
    for d, z in peers:
        pl.semaphore_signal(barrier, inc=1, device_id=where_is(d, z), device_id_type=pl.DeviceIdType.MESH)
    pl.semaphore_wait(barrier, len(peers))
    load_t.wait()
    load_c.wait()

    def rcopy(src, dst, ssem, rsem, d, z):
        return pltpu.make_async_remote_copy(
            src_ref=src, dst_ref=dst, send_sem=ssem, recv_sem=rsem,
            device_id=where_is(d, z), device_id_type=pl.DeviceIdType.MESH,
        )

    pending = []

    def begin(copy, pred=None):
        if pred is None:
            copy.start()
        else:
            pl.when(pred)(copy.start)
        pending.append((copy, pred))

    def both(a, b):
        return b if a is None else (a if b is None else jnp.logical_and(a, b))

    def slot_copy(slot, ssem, d, z, half=None):
        view = buf.at[slot] if half is None else buf.at[slot, half]
        return rcopy(view, view, ssem, agr.at[slot, half or 0], d, z)

    order = [(0, 0)]
    for k in range(1, experts):
        order += [(k, -1), (k, 1)]

    def origin(k, side):
        z = ex + side * k
        if k == 0:
            return z, None
        return z, (z >= 0 if side < 0 else z < experts)

    def sidx(k, side):
        return 2 * k + (1 if side > 0 else 0)

    def z_step(k, side):
        z, ok = origin(k, side)
        slot = dp * experts + z
        i = sidx(k, side)
        if k:
            pl.when(ok)(slot_copy(slot, zs.at[i, 0], dp, ex).wait_recv)
        if side <= 0:
            begin(slot_copy(slot, zs.at[i, 0], dp, ex + 1), both(ok, ex + 1 < experts))
        if side >= 0:
            begin(slot_copy(slot, zs.at[i, 1], dp, ex - 1), both(ok, ex > 0))
        begin(slot_copy(slot, xs.at[i], dp_x, ex), ok)
        begin(slot_copy(slot, ys.at[i], dp_y, ex), ok)
        begin(slot_copy(slot, cs.at[i, 0], dp_c, ex), ok)

    def guarded(ok, fn):
        if ok is None:
            fn()
        else:
            pl.when(ok)(fn)

    def xy_step(k, side):
        z, ok = origin(k, side)
        i = sidx(k, side)
        slot = dp_x * experts + z
        guarded(ok, slot_copy(slot, xs.at[i], dp_x, ex).wait_recv)
        begin(slot_copy(slot, dys.at[i], dp_y, ex, 0), ok)
        begin(slot_copy(slot, cs.at[i, 1], dp_c, ex), ok)
        slot = dp_y * experts + z
        guarded(ok, slot_copy(slot, ys.at[i], dp_y, ex).wait_recv)
        begin(slot_copy(slot, dxs.at[i], dp_x, ex, 1), ok)
        begin(slot_copy(slot, cs.at[i, 2], dp_c, ex), ok)

    def diag_step(k, side):
        z, ok = origin(k, side)
        i = sidx(k, side)
        slot = dp_d * experts + z
        guarded(ok, slot_copy(slot, dys.at[i], dp_y, ex, 0).wait_recv)
        guarded(ok, slot_copy(slot, dxs.at[i], dp_x, ex, 1).wait_recv)
        begin(slot_copy(slot, cs.at[i, 3], dp_c, ex), ok)

    for k in range(experts + 2):
        for kk, side in order:
            if kk == k:
                z_step(kk, side)
        for kk, side in order:
            if kk == k - 1:
                xy_step(kk, side)
        for kk, side in order:
            if kk == k - 2:
                diag_step(kk, side)
    for kk, side in order:
        z, ok = origin(kk, side)
        for d in (dp_c, dp_x + to_core, dp_y + to_core, dp_d + to_core):
            guarded(ok, slot_copy(d * experts + z, cs.at[0, 0], dp_c, ex).wait_recv)

    gain = gain_ref[...]

    def prepare(j, carry):
        rows = pl.ds(pl.multiple_of(j * 2 * tok_count, 2 * tok_count), 2 * tok_count)
        x = buf[pl.ds(2 * j, 2), 0, :, 0:width].astype(F32).reshape(2 * tok_count, width)
        inverse = 1.0 / jnp.sqrt(jnp.mean(x * x, axis=-1, keepdims=True) + EPSILON)
        normed = x * inverse
        norm[rows, :] = normed
        inv[rows, :] = jnp.broadcast_to(inverse, (2 * tok_count, 128))
        tok[rows, :] = x.astype(BF16)
        hid[rows, :] = (normed * gain).astype(BF16)
        c = buf[pl.ds(2 * j, 2), 1, :, 0:width].astype(F32).reshape(2 * tok_count, width)
        cot[rows, :] = c.astype(BF16)
        wcol[rows, :] = buf[pl.ds(2 * j, 2), 0, :, width : width + 128].astype(F32).reshape(2 * tok_count, 128)
        return carry

    lax.fori_loop(0, blocks // 2, prepare, 0)

    router = router_ref[...]
    store_split(rsp, router)
    logits = join_split(
        lax.dot_general(rsp[...].astype(BF16), hid[...], NT, preferred_element_type=F32), experts
    )
    pick_rows = wcol[...].T
    first, second = pick_rows[0:1, :], pick_rows[1:2, :]
    ids = lax.broadcasted_iota(jnp.int32, (experts, total), 0).astype(F32)
    first_hot = (first == ids).astype(F32)
    second_hot = (second == ids).astype(F32)
    gate_first = jax.nn.sigmoid(
        jnp.sum(logits * first_hot, 0, keepdims=True) - jnp.sum(logits * second_hot, 0, keepdims=True)
    )
    gate_second = 1.0 - gate_first
    here = ex.astype(F32)
    mine_first = (first == here).astype(F32)
    mine_second = (second == here).astype(F32)
    weight = gate_first * mine_first + gate_second * mine_second
    wcol[...] = jnp.broadcast_to(weight, (128, total)).T

    pick = jnp.zeros((total, 1), F32)
    for t in range(4):
        for cp in wcopies[t]:
            cp.wait()
        a, b = t * tile, (t + 1) * tile
        pre_gate = jnp.dot(hid[...], wg[:, a:b], preferred_element_type=F32)
        pre_up = jnp.dot(hid[...], wu[:, a:b], preferred_element_type=F32)
        back = lax.dot_general(cot[...], wd[a:b, :], NT, preferred_element_type=F32)
        s = jax.nn.sigmoid(pre_gate)
        silu = pre_gate * s
        act = (silu * pre_up).astype(BF16).astype(F32)
        pick = pick + jnp.sum(act * back, -1, keepdims=True)
        dg[:, a:b] = (back * pre_up * (s + silu * (1.0 - s))).astype(BF16)
        du[:, a:b] = (back * silu).astype(BF16)
    pick_row = jnp.broadcast_to(pick, (total, 128)).T[0:1, :]
    vsrc[:, width : width + total] = pick_row * (mine_first - mine_second)

    step = width // 4
    for n in range(4):
        a, b = n * step, (n + 1) * step
        part = lax.dot_general(dg[...], wg[a:b, :], NT, preferred_element_type=F32)
        part = part + lax.dot_general(du[...], wu[a:b, :], NT, preferred_element_type=F32)
        part = part * jnp.concatenate([wcol[...]] * (step // 128), axis=1)
        vsrc[:, a:b] = jnp.sum(part * norm[:, a:b], axis=0, keepdims=True)
        pbuf[:, :, a:b] = part.reshape(blocks, tok_count, step).astype(BF16)

    g_of = [group + to_x + to_y, group + to_x, group + to_y, group]
    vcore = rcopy(vsrc, cvec, vs.at[0], vr.at[0], dp_c, ex)
    halves = []
    for i, g in enumerate(g_of):
        src = pbuf.at[pl.ds((2 * g + 1 - core) * experts, experts)]
        halves.append(rcopy(src, cbuf.at[i], rs_s.at[i], rs_r.at[i], dp_c, ex))
    begin(halves[0])
    begin(vcore)
    for h in halves[1:]:
        begin(h)
    planes = []
    for i, d in enumerate((dp_d, dp_x, dp_y)):
        halves[i].wait_recv()
        own = pbuf[pl.ds((2 * g_of[i] + core) * experts, experts)].astype(F32)
        sbuf[i] = (own + cbuf[i].astype(F32)).astype(BF16)
        cp = rcopy(sbuf.at[i], plbuf.at[i], pl_s.at[i], pl_r.at[i], d, ex)
        begin(cp)
        planes.append(cp)
        if i == 0:
            vcore.wait_recv()
            vchip[...] = vsrc[...] + cvec[...]
            vplanes = []
            for j, dd in enumerate((dp_d, dp_x, dp_y)):
                vp = rcopy(vchip, pvec.at[j], vs.at[1 + j], vr.at[1 + j], dd, ex)
                begin(vp)
                vplanes.append(vp)
    for vp in vplanes:
        vp.wait_recv()
    vplane[...] = (vchip[...] + pvec[1]) + (pvec[2] + pvec[0])
    zvec[ex] = vplane[...]
    vz = []
    for k in range(1, experts):
        z = lax.rem(ex + k, experts)
        cp = rcopy(vplane, zvec.at[ex], vs.at[4 + k], vr.at[4 + ex], dp, z)
        begin(cp)
    halves[3].wait_recv()
    for cp in planes:
        cp.wait_recv()
    own_base = (2 * group + core) * experts

    def plane_sum(z):
        v = pbuf[own_base + z].astype(F32) + cbuf[3, z].astype(F32)
        for i in range(3):
            v = v + plbuf[i, z].astype(F32)
        return v

    for k in (2, 1, 3) if experts == 4 else range(1, experts):
        z = lax.rem(ex + k, experts)
        zsrc[z] = plane_sum(z).astype(BF16)
        begin(rcopy(zsrc.at[z], zbuf.at[ex], zz_s.at[k], zz_r.at[ex], dp, z))
    hidden_grad = plane_sum(ex)

    for k in range(1, experts):
        z = lax.rem(ex + k, experts)
        rcopy(vplane, zvec.at[z], vs.at[4 + k], vr.at[4 + z], dp, z).wait_recv()
    vec = zvec[0]
    for z in range(1, experts):
        vec = vec + zvec[z]
    gate_delta = gate_first * gate_second * vec[:, width : width + total]
    logit_grad = (first_hot - second_hot) * gate_delta
    store_split(lsp, logit_grad)
    inv_row = inv[...].T[0:1, :]
    store_split(lspi, logit_grad * inv_row)
    out_router[...] = join_split(jnp.dot(lsp[...].astype(BF16), hid[...], preferred_element_type=F32), experts)
    by_norm = join_split(jnp.dot(lspi[...].astype(BF16), tok[...], preferred_element_type=F32), experts)
    out_gain[...] = vec[:, 0:width] + jnp.sum(by_norm * router, axis=0, keepdims=True)
    lanes = lax.broadcasted_iota(jnp.int32, (128, total), 0)
    spread = jnp.zeros((128, total), F32)
    for e in range(experts):
        spread = jnp.where(lanes == e, logit_grad[e : e + 1, :], spread)
    lgcol[...] = spread.T
    rows = pl.ds(pl.multiple_of(me * tok_count, tok_count), tok_count)
    mine = lgcol[rows, :]
    for e in range(experts):
        hidden_grad = hidden_grad + mine[:, e : e + 1] * router[e : e + 1, :]
    for k in range(1, experts):
        z = lax.rem(ex + k, experts)
        rcopy(zsrc.at[z], zbuf.at[z], zz_s.at[k], zz_r.at[z], dp, z).wait_recv()
        hidden_grad = hidden_grad + zbuf[z].astype(F32)
    scaled = hidden_grad * gain
    normed = norm[rows, :]
    grad = buf[me, 1, :, 0:width].astype(F32) + inv[rows, 0:1] * (
        scaled - normed * jnp.mean(scaled * normed, axis=-1, keepdims=True)
    )
    out_tok[...] = grad.astype(BF16)
    for cp, pred in pending:
        guarded(pred, cp.wait_send)


def dense(tokens, cotangent, expert_picks, w_gate, w_up, w_down, router, norm_gain):
    experts = lax.axis_size("expert")
    groups = lax.axis_size("dp")
    t, width = tokens.shape
    ff = w_gate.shape[2]
    blocks = experts * groups
    total = blocks * t
    plane = groups // 2
    steps = 2 * experts
    vec = width + total
    dma = pltpu.SemaphoreType.DMA
    vmem = pltpu.VMEM
    scratch = [
        vmem((blocks, 2, t, width + 128), BF16),
        vmem((width, ff), BF16), vmem((width, ff), BF16), vmem((ff, width), BF16),
        vmem((total, width), BF16), vmem((total, width), BF16), vmem((total, width), BF16),
        vmem((total, width), F32), vmem((total, 128), F32),
        vmem((total, ff), BF16), vmem((total, ff), BF16),
        vmem((total, 128), F32), vmem((total, 128), F32),
        vmem((32, width), F32), vmem((32, total), F32), vmem((32, total), F32),
        vmem((blocks, t, width), BF16), vmem((plane, experts, t, width), BF16),
        vmem((plane - 1, experts, t, width), BF16), vmem((plane - 1, experts, t, width), BF16),
        vmem((experts, t, width), BF16), vmem((experts, t, width), BF16),
        vmem((total, 128), F32),
        vmem((1, vec), F32), vmem((1, vec), F32), vmem((1, vec), F32), vmem((3, 1, vec), F32),
        vmem((1, vec), F32), vmem((experts, 1, vec), F32),
        dma((2,)), dma((12,)), dma((blocks, 2)), dma((steps, 2)), dma((steps,)), dma((steps,)),
        dma((steps, 4)), dma((steps,)), dma((steps,)),
        dma((4,)), dma((4,)), dma((3,)), dma((3,)), dma((experts,)), dma((experts,)),
        dma((4 + experts,)), dma((4 + experts,)),
    ]
    inside = pl.BlockSpec(memory_space=pltpu.VMEM)
    outside = pl.BlockSpec(memory_space=pl.ANY)
    grad, router_grad, gain_grad = pl.pallas_call(
        functools.partial(dense_kernel, experts),
        out_shape=(
            jax.ShapeDtypeStruct((t, width), BF16),
            jax.ShapeDtypeStruct((experts, width), F32),
            jax.ShapeDtypeStruct((1, width), F32),
        ),
        in_specs=[outside, outside, inside, outside, outside, outside, inside, inside],
        out_specs=(inside, inside, inside),
        scratch_shapes=scratch,
        compiler_params=pltpu.CompilerParams(
            collective_id=0, has_side_effects=True, vmem_limit_bytes=60 * 2**20
        ),
    )(tokens, cotangent, expert_picks, w_gate, w_up, w_down, router, norm_gain.reshape(1, width))
    return grad, router_grad, gain_grad.reshape(width)


def local(tokens, cotangent, expert_picks, w_gate, w_up, w_down, router, norm_gain):
    experts = lax.axis_size("expert")
    groups = lax.axis_size("dp")
    tok_count = tokens.shape[0]
    feature_width = tokens.shape[1]
    capacity = 4 * tok_count // experts
    gate_shard = w_gate[0]
    up_shard = w_up[0]
    down_shard = w_down[0]
    x_float = tokens.astype(jnp.float32)
    inverse = 1.0 / jnp.sqrt(jnp.mean(x_float * x_float, axis=-1, keepdims=True) + EPSILON)
    normed = x_float * inverse
    hidden = (normed * norm_gain).astype(jnp.bfloat16)
    hidden_float = hidden.astype(jnp.float32)
    logits = lax.dot_general(
        hidden_float, router, (((1,), (1,)), ((), ())), precision=highest_precision
    )
    expert_ids = jnp.arange(experts, dtype=jnp.int32)
    first_hot = (expert_picks[:, 0:1] == expert_ids).astype(jnp.float32)
    second_hot = (expert_picks[:, 1:2] == expert_ids).astype(jnp.float32)
    gate_first = jax.nn.sigmoid(jnp.sum(logits * first_hot, -1) - jnp.sum(logits * second_hot, -1))
    gate_second = 1.0 - gate_first
    pair_expert = expert_picks.reshape(-1)
    pair_hot = (pair_expert[:, None] == expert_ids).astype(jnp.int32)
    slot_rank = jnp.sum(jnp.cumsum(pair_hot, axis=0) * pair_hot, axis=1) - 1
    empty_slots = jnp.zeros((experts, capacity, feature_width), jnp.bfloat16)
    send_rows = empty_slots.at[pair_expert, slot_rank].set(jnp.repeat(hidden, 2, axis=0))
    send_cots = empty_slots.at[pair_expert, slot_rank].set(jnp.repeat(cotangent, 2, axis=0))
    arrived_rows, arrived_cots = (
        lax.all_to_all(send_rows, "expert", split_axis=0, concat_axis=0, tiled=True),
        lax.all_to_all(send_cots, "expert", split_axis=0, concat_axis=0, tiled=True),
    )
    group_rows, group_cots = (
        lax.all_gather(arrived_rows, "dp", axis=0, tiled=True),
        lax.all_gather(arrived_cots, "dp", axis=0, tiled=True),
    )
    d_rows, pick_part = expert_pass(
        group_rows.reshape(-1, feature_width),
        group_cots.reshape(-1, feature_width),
        gate_shard,
        up_shard,
        down_shard,
    )
    pick_grid = pick_part.reshape(groups, experts, capacity)
    summed = lax.psum_scatter(
        d_rows.reshape(groups * experts, capacity, feature_width).astype(jnp.bfloat16),
        "dp",
        scatter_dimension=0,
        tiled=True,
    )
    grad_back = lax.all_to_all(summed, "expert", split_axis=0, concat_axis=0, tiled=True)
    column_hot = (expert_ids == lax.axis_index("expert")).astype(jnp.float32)
    pick_table = pick_grid[:, :, None, :] * column_hot[None, None, :, None]
    pick_total = lax.psum(pick_table, ("dp", "expert"))
    pick_mine = pick_total[lax.axis_index("dp"), lax.axis_index("expert")]
    pick_inner = pick_mine[pair_expert, slot_rank].reshape(tok_count, 2)
    grad_pairs = (
        grad_back[pair_expert, slot_rank].astype(jnp.float32).reshape(tok_count, 2, feature_width)
    )
    gate_delta = gate_first * gate_second * (pick_inner[:, 0] - pick_inner[:, 1])
    logit_grad = (first_hot - second_hot) * gate_delta[:, None]
    hidden_grad = gate_first[:, None] * grad_pairs[:, 0] + gate_second[:, None] * grad_pairs[:, 1]
    hidden_grad = hidden_grad + jnp.dot(logit_grad, router, precision=highest_precision)
    router_part = lax.dot_general(
        logit_grad, hidden_float, (((0,), (0,)), ((), ())), precision=highest_precision
    )
    gain_part = jnp.sum(hidden_grad * normed, axis=0)
    router_grad, gain_grad = lax.psum((router_part, gain_part), ("dp", "expert"))
    scaled_grad = hidden_grad * norm_gain
    token_grad = cotangent.astype(jnp.float32) + inverse * (
        scaled_grad - normed * jnp.mean(scaled_grad * normed, axis=-1, keepdims=True)
    )
    return (token_grad.astype(jnp.bfloat16), router_grad, gain_grad)


def solution(mesh):
    in_specs = (
        P(("dp", "expert"), None),
        P(("dp", "expert"), None),
        P(("dp", "expert"), None),
        P("expert", None, "dp"),
        P("expert", None, "dp"),
        P("expert", "dp", None),
        P(),
        P(),
    )
    out_specs = (P(("dp", "expert"), None), P(), P())
    groups, experts = mesh.shape["dp"], mesh.shape["expert"]
    body = dense if experts <= 4 and groups == 2**3 else local
    return jax.shard_map(body, mesh=mesh, in_specs=in_specs, out_specs=out_specs, check_vma=False)
```

```python
import functools

import jax
import jax.numpy as jnp
from jax import lax
from jax.experimental import pallas as pl
from jax.experimental.pallas import tpu as pltpu
from jax.sharding import PartitionSpec as P

EPSILON = 1e-05
highest_precision = lax.Precision.HIGHEST


def silu_grad(pre_act):
    sigmoid_value = jax.nn.sigmoid(pre_act)
    return sigmoid_value + pre_act * sigmoid_value * (1.0 - sigmoid_value)


def expert_pass(slot_rows, slot_cots, gate_shard, up_shard, down_shard):
    pre_gate = jnp.dot(slot_rows, gate_shard, preferred_element_type=jnp.float32)
    pre_up = jnp.dot(slot_rows, up_shard, preferred_element_type=jnp.float32)
    act = (jax.nn.silu(pre_gate) * pre_up).astype(jnp.bfloat16)
    cot_back = lax.dot_general(
        slot_cots, down_shard, (((1,), (1,)), ((), ())), preferred_element_type=jnp.float32
    )
    pick_part = jnp.sum(act.astype(jnp.float32) * cot_back, -1)
    d_gate = (cot_back * pre_up * silu_grad(pre_gate)).astype(jnp.bfloat16)
    d_up = (cot_back * jax.nn.silu(pre_gate)).astype(jnp.bfloat16)
    d_rows = lax.dot_general(
        d_gate, gate_shard, (((1,), (1,)), ((), ())), preferred_element_type=jnp.float32
    )
    d_rows = d_rows + lax.dot_general(
        d_up, up_shard, (((1,), (1,)), ((), ())), preferred_element_type=jnp.float32
    )
    return (d_rows, pick_part)


NT = (((1,), (1,)), ((), ()))
F32 = jnp.float32
BF16 = jnp.bfloat16


def split3(v):
    hi = v.astype(BF16).astype(F32)
    mid = (v - hi).astype(BF16).astype(F32)
    return hi, mid, v - hi - mid


def store_split(ref, v):
    n = v.shape[0]
    ref[...] = jnp.zeros_like(ref)
    for i, part in enumerate(split3(v)):
        ref[8 * i : 8 * i + n, :] = part


def join_split(v, n):
    return v[0:n] + v[8 : 8 + n] + v[16 : 16 + n]


def dense_kernel(
    experts, tok_ref, cot_ref, picks_ref, wg_hbm, wu_hbm, wd_hbm, router_ref, gain_ref,
    out_tok, out_router, out_gain,
    buf, wg, wu, wd, hid, tok, cot, norm, inv, dg, du, wcol, lgcol, rsp, lsp, lspi,
    pbuf, cbuf, sbuf, plbuf, zsrc, zbuf, pickcol, vsrc, cvec, vchip, pvec, vplane, zvec,
    lsem, wsem, agr, zs, xs, ys, cs, dxs, dys, rs_s, rs_r, pl_s, pl_r, zz_s, zz_r, vs, vr,
):
    width = tok_ref.shape[1]
    tok_count = tok_ref.shape[0]
    blocks = buf.shape[0]
    total = blocks * tok_count
    ff = wg.shape[1]
    dp = lax.axis_index("dp")
    ex = lax.axis_index("expert")
    core = lax.rem(dp, 2)
    group = lax.div(dp, 2)
    xbit = lax.rem(group, 2)
    ybit = lax.div(group, 2)
    to_core = 1 - 2 * core
    to_x = 1 - 2 * xbit
    to_y = 2 * (1 - 2 * ybit)
    dp_c = dp + to_core
    dp_x = dp + 2 * to_x
    dp_y = dp + 2 * to_y
    dp_d = dp + 2 * (to_x + to_y)
    me = dp * experts + ex

    tile = ff // 4
    wcopies = []
    for t in range(4):
        part = pl.ds(t * tile, tile)
        three = (
            pltpu.make_async_copy(wg_hbm.at[0, :, part], wg.at[:, part], wsem.at[3 * t]),
            pltpu.make_async_copy(wu_hbm.at[0, :, part], wu.at[:, part], wsem.at[3 * t + 1]),
            pltpu.make_async_copy(wd_hbm.at[0, part, :], wd.at[part, :], wsem.at[3 * t + 2]),
        )
        wcopies.append(three)
    load_t = pltpu.make_async_copy(tok_ref, buf.at[me, 0, :, pl.ds(0, width)], lsem.at[0])
    load_c = pltpu.make_async_copy(cot_ref, buf.at[me, 1, :, pl.ds(0, width)], lsem.at[1])
    load_t.start()
    load_c.start()
    picks = picks_ref[...].astype(F32)
    lane = lax.broadcasted_iota(jnp.int32, (tok_count, 128), 1)
    diagonal = lax.broadcasted_iota(jnp.int32, (tok_count, tok_count), 0) == lax.broadcasted_iota(
        jnp.int32, (tok_count, tok_count), 1
    )
    first_pick = jnp.sum(jnp.where(diagonal, picks[0:1, :], 0.0), axis=1, keepdims=True)
    second_pick = jnp.sum(jnp.where(diagonal, picks[1:2, :], 0.0), axis=1, keepdims=True)
    picks_tile = jnp.where(lane == 0, first_pick, jnp.where(lane == 1, second_pick, 0.0))
    buf[me, 0, :, width : width + 128] = picks_tile.astype(BF16)
    buf[me, 1, :, width : width + 128] = jnp.zeros((tok_count, 128), BF16)
    for three in wcopies:
        for cp in three:
            cp.start()

    def where_is(d, z):
        return {"dp": d, "expert": z}

    barrier = pltpu.get_barrier_semaphore()
    def greet(d, z):
        pl.semaphore_signal(barrier, inc=1, device_id=where_is(d, z), device_id_type=pl.DeviceIdType.MESH)

    for d in (dp_c, dp_x, dp_y):
        greet(d, ex)
    pl.when(ex > 0)(lambda: greet(dp, ex - 1))
    pl.when(ex + 1 < experts)(lambda: greet(dp, ex + 1))
    pl.semaphore_wait(barrier, 3 + jnp.minimum(ex, 1) + jnp.minimum(experts - 1 - ex, 1))
    load_t.wait()
    load_c.wait()

    def rcopy(src, dst, ssem, rsem, d, z):
        return pltpu.make_async_remote_copy(
            src_ref=src, dst_ref=dst, send_sem=ssem, recv_sem=rsem,
            device_id=where_is(d, z), device_id_type=pl.DeviceIdType.MESH,
        )

    pending = []

    def begin(copy, pred=None):
        if pred is None:
            copy.start()
        else:
            pl.when(pred)(copy.start)
        pending.append((copy, pred))

    def both(a, b):
        return b if a is None else (a if b is None else jnp.logical_and(a, b))

    def slot_copy(slot, ssem, d, z, half):
        view = buf.at[slot, half]
        return rcopy(view, view, ssem, agr.at[slot, half], d, z)

    order = [(0, 0)]
    for k in range(1, experts):
        order += [(k, -1), (k, 1)]

    def origin(k, side):
        z = ex + side * k
        if k == 0:
            return z, None
        return z, (z >= 0 if side < 0 else z < experts)

    def sidx(k, side):
        return 2 * k + (1 if side > 0 else 0)

    def guarded(ok, fn):
        if ok is None:
            fn()
        else:
            pl.when(ok)(fn)

    def z_step(k, side, half):
        z, ok = origin(k, side)
        slot = dp * experts + z
        i = sidx(k, side)
        if k:
            pl.when(ok)(slot_copy(slot, zs.at[i, 0, half], dp, ex, half).wait_recv)
        if side <= 0:
            begin(slot_copy(slot, zs.at[i, 0, half], dp, ex + 1, half), both(ok, ex + 1 < experts))
        if side >= 0:
            begin(slot_copy(slot, zs.at[i, 1, half], dp, ex - 1, half), both(ok, ex > 0))
        begin(slot_copy(slot, xs.at[i, half], dp_x, ex, half), ok)
        begin(slot_copy(slot, ys.at[i, half], dp_y, ex, half), ok)
        begin(slot_copy(slot, cs.at[i, 0, half], dp_c, ex, half), ok)

    def xy_step(k, side):
        z, ok = origin(k, side)
        i = sidx(k, side)
        from_x = dp_x * experts + z
        from_y = dp_y * experts + z
        guarded(ok, slot_copy(from_x, xs.at[i, 0], dp_x, ex, 0).wait_recv)
        begin(slot_copy(from_x, dys.at[i], dp_y, ex, 0), ok)
        begin(slot_copy(from_x, cs.at[i, 1, 0], dp_c, ex, 0), ok)
        guarded(ok, slot_copy(from_y, ys.at[i, 1], dp_y, ex, 1).wait_recv)
        begin(slot_copy(from_y, dxs.at[i], dp_x, ex, 1), ok)
        begin(slot_copy(from_y, cs.at[i, 2, 1], dp_c, ex, 1), ok)
        guarded(ok, slot_copy(from_x, xs.at[i, 1], dp_x, ex, 1).wait_recv)
        begin(slot_copy(from_x, cs.at[i, 1, 1], dp_c, ex, 1), ok)
        guarded(ok, slot_copy(from_y, ys.at[i, 0], dp_y, ex, 0).wait_recv)
        begin(slot_copy(from_y, cs.at[i, 2, 0], dp_c, ex, 0), ok)

    def diag_step(k, side):
        z, ok = origin(k, side)
        i = sidx(k, side)
        slot = dp_d * experts + z
        guarded(ok, slot_copy(slot, dys.at[i], dp_y, ex, 0).wait_recv)
        begin(slot_copy(slot, cs.at[i, 3, 0], dp_c, ex, 0), ok)
        guarded(ok, slot_copy(slot, dxs.at[i], dp_x, ex, 1).wait_recv)
        begin(slot_copy(slot, cs.at[i, 3, 1], dp_c, ex, 1), ok)

    gain = gain_ref[...]

    def prepare(j, carry):
        rows = pl.ds(pl.multiple_of(j * 2 * tok_count, 2 * tok_count), 2 * tok_count)
        x = buf[pl.ds(2 * j, 2), 0, :, 0:width].astype(F32).reshape(2 * tok_count, width)
        inverse = 1.0 / jnp.sqrt(jnp.mean(x * x, axis=-1, keepdims=True) + EPSILON)
        normed = x * inverse
        norm[rows, :] = normed
        inv[rows, :] = jnp.broadcast_to(inverse, (2 * tok_count, 128))
        tok[rows, :] = x.astype(BF16)
        hid[rows, :] = (normed * gain).astype(BF16)
        c = buf[pl.ds(2 * j, 2), 1, :, 0:width].astype(F32).reshape(2 * tok_count, width)
        cot[rows, :] = c.astype(BF16)
        wcol[rows, :] = buf[pl.ds(2 * j, 2), 0, :, width : width + 128].astype(F32).reshape(2 * tok_count, 128)
        return carry

    def prepare_rows(d):
        pairs = experts // 2
        lax.fori_loop(0, pairs, lambda i, carry: prepare(d * pairs + i, carry), 0)

    for k in range(experts + 2):
        for half in range(2):
            for kk, side in order:
                if kk == k:
                    z_step(kk, side, half)
        for kk, side in order:
            if kk == k - 1:
                xy_step(kk, side)
        for kk, side in order:
            if kk == k - 2:
                diag_step(kk, side)
        if k == experts:
            for d in (dp, dp_x, dp_y):
                prepare_rows(d)
    prepare_rows(dp_d)
    for d in (dp_c, dp_x + to_core, dp_y + to_core, dp_d + to_core):
        for z in range(experts):
            for half in range(2):
                slot_copy(d * experts + z, cs.at[0, 0, 0], dp_c, ex, half).wait_recv()
        prepare_rows(d)


    router = router_ref[...]
    store_split(rsp, router)
    logits = join_split(
        lax.dot_general(rsp[...].astype(BF16), hid[...], NT, preferred_element_type=F32), experts
    )
    pick_rows = wcol[...].T
    first, second = pick_rows[0:1, :], pick_rows[1:2, :]
    ids = lax.broadcasted_iota(jnp.int32, (experts, total), 0).astype(F32)
    first_hot = (first == ids).astype(F32)
    second_hot = (second == ids).astype(F32)
    gate_first = jax.nn.sigmoid(
        jnp.sum(logits * first_hot, 0, keepdims=True) - jnp.sum(logits * second_hot, 0, keepdims=True)
    )
    gate_second = 1.0 - gate_first
    here = ex.astype(F32)
    mine_first = (first == here).astype(F32)
    mine_second = (second == here).astype(F32)
    weight = gate_first * mine_first + gate_second * mine_second
    wcol[...] = jnp.broadcast_to(weight, (128, total)).T

    pick = jnp.zeros((total, 1), F32)
    for t in range(4):
        for cp in wcopies[t]:
            cp.wait()
        a, b = t * tile, (t + 1) * tile
        pre_gate = jnp.dot(hid[...], wg[:, a:b], preferred_element_type=F32)
        pre_up = jnp.dot(hid[...], wu[:, a:b], preferred_element_type=F32)
        back = lax.dot_general(cot[...], wd[a:b, :], NT, preferred_element_type=F32)
        s = jax.nn.sigmoid(pre_gate)
        silu = pre_gate * s
        act = (silu * pre_up).astype(BF16).astype(F32)
        pick = pick + jnp.sum(act * back, -1, keepdims=True)
        dg[:, a:b] = (back * pre_up * (s + silu * (1.0 - s))).astype(BF16)
        du[:, a:b] = (back * silu).astype(BF16)
    pick_row = jnp.broadcast_to(pick, (total, 128)).T[0:1, :]
    vsrc[:, width : width + total] = pick_row * (mine_first - mine_second)

    chunks = pbuf.shape[0]
    wide = width // chunks
    step = wide // 2

    def backward(c, h):
        a = c * wide + h * step
        part = lax.dot_general(dg[...], wg[a : a + step, :], NT, preferred_element_type=F32)
        part = part + lax.dot_general(du[...], wu[a : a + step, :], NT, preferred_element_type=F32)
        part = part * jnp.concatenate([wcol[...]] * (step // 128), axis=1)
        vsrc[:, a : a + step] = jnp.sum(part * norm[:, a : a + step], axis=0, keepdims=True)
        pbuf[c, :, :, h * step : (h + 1) * step] = part.reshape(blocks, tok_count, step).astype(BF16)

    g_of = [group + to_x + to_y, group + to_x, group + to_y, group]
    halves = {}
    planes = {}

    def core_stage(c):
        for i, g in enumerate(g_of):
            src = pbuf.at[c, pl.ds((2 * g + 1 - core) * experts, experts)]
            halves[c, i] = rcopy(src, cbuf.at[c, i], rs_s.at[c, i], rs_r.at[c, i], dp_c, ex)
            begin(halves[c, i])

    def plane_stage(c):
        for i, d in enumerate((dp_d, dp_x, dp_y)):
            halves[c, i].wait_recv()
            own = pbuf[c, pl.ds((2 * g_of[i] + core) * experts, experts)].astype(F32)
            sbuf[c, i] = (own + cbuf[c, i].astype(F32)).astype(BF16)
            planes[c, i] = rcopy(sbuf.at[c, i], plbuf.at[c, i], pl_s.at[c, i], pl_r.at[c, i], d, ex)
            begin(planes[c, i])

    own_base = (2 * group + core) * experts

    def plane_sum(c, z):
        v = pbuf[c, own_base + z].astype(F32) + cbuf[c, 3, z].astype(F32)
        for i in range(3):
            v = v + plbuf[c, i, z].astype(F32)
        return v

    def z_stage(c):
        halves[c, 3].wait_recv()
        for i in range(3):
            planes[c, i].wait_recv()
        for k in range(1, experts):
            z = lax.rem(ex + k, experts)
            zsrc[c, z] = plane_sum(c, z).astype(BF16)
            begin(rcopy(zsrc.at[c, z], zbuf.at[c, ex], zz_s.at[c, k], zz_r.at[c, ex], dp, z))
        return plane_sum(c, ex)

    backward(0, 0)
    backward(0, 1)
    core_stage(0)
    backward(1, 0)
    plane_stage(0)
    backward(1, 1)
    core_stage(1)
    vcore = rcopy(vsrc, cvec, vs.at[0], vr.at[0], dp_c, ex)
    begin(vcore)
    plane_stage(1)
    vcore.wait_recv()
    vchip[...] = vsrc[...] + cvec[...]
    vplanes = []
    for j, dd in enumerate((dp_d, dp_x, dp_y)):
        vp = rcopy(vchip, pvec.at[j], vs.at[1 + j], vr.at[1 + j], dd, ex)
        begin(vp)
        vplanes.append(vp)
    sums = [z_stage(0)]
    for vp in vplanes:
        vp.wait_recv()
    vplane[...] = (vchip[...] + pvec[1]) + (pvec[2] + pvec[0])
    zvec[ex] = vplane[...]
    for k in range(1, experts):
        z = lax.rem(ex + k, experts)
        begin(rcopy(vplane, zvec.at[ex], vs.at[4 + k], vr.at[4 + ex], dp, z))
    sums.append(z_stage(1))
    hidden_grad = jnp.concatenate(sums, axis=1)

    for k in range(1, experts):
        z = lax.rem(ex + k, experts)
        rcopy(vplane, zvec.at[z], vs.at[4 + k], vr.at[4 + z], dp, z).wait_recv()
    vec = zvec[0]
    for z in range(1, experts):
        vec = vec + zvec[z]
    gate_delta = gate_first * gate_second * vec[:, width : width + total]
    logit_grad = (first_hot - second_hot) * gate_delta
    store_split(lsp, logit_grad)
    inv_row = inv[...].T[0:1, :]
    store_split(lspi, logit_grad * inv_row)
    out_router[...] = join_split(jnp.dot(lsp[...].astype(BF16), hid[...], preferred_element_type=F32), experts)
    by_norm = join_split(jnp.dot(lspi[...].astype(BF16), tok[...], preferred_element_type=F32), experts)
    out_gain[...] = vec[:, 0:width] + jnp.sum(by_norm * router, axis=0, keepdims=True)
    lanes = lax.broadcasted_iota(jnp.int32, (128, total), 0)
    spread = jnp.zeros((128, total), F32)
    for e in range(experts):
        spread = jnp.where(lanes == e, logit_grad[e : e + 1, :], spread)
    lgcol[...] = spread.T
    rows = pl.ds(pl.multiple_of(me * tok_count, tok_count), tok_count)
    mine = lgcol[rows, :]
    for e in range(experts):
        hidden_grad = hidden_grad + mine[:, e : e + 1] * router[e : e + 1, :]
    for k in range(1, experts):
        z = lax.rem(ex + k, experts)
        arrived = []
        for c in range(chunks):
            rcopy(zsrc.at[c, z], zbuf.at[c, z], zz_s.at[c, k], zz_r.at[c, z], dp, z).wait_recv()
            arrived.append(zbuf[c, z].astype(F32))
        hidden_grad = hidden_grad + jnp.concatenate(arrived, axis=1)
    scaled = hidden_grad * gain
    normed = norm[rows, :]
    grad = buf[me, 1, :, 0:width].astype(F32) + inv[rows, 0:1] * (
        scaled - normed * jnp.mean(scaled * normed, axis=-1, keepdims=True)
    )
    out_tok[...] = grad.astype(BF16)
    for cp, pred in pending:
        guarded(pred, cp.wait_send)


def hand_on(a_in, b_in, c_in, a_out, b_out, c_out):
    a_out[...] = a_in[...]
    b_out[...] = b_in[...]
    c_out[...] = c_in[...]


def dense(tokens, cotangent, expert_picks, w_gate, w_up, w_down, router, norm_gain):
    experts = lax.axis_size("expert")
    groups = lax.axis_size("dp")
    t, width = tokens.shape
    ff = w_gate.shape[2]
    blocks = experts * groups
    total = blocks * t
    plane = groups // 2
    steps = 2 * experts
    vec = width + total
    wide = width // 2
    dma = pltpu.SemaphoreType.DMA
    vmem = pltpu.VMEM
    scratch = [
        vmem((blocks, 2, t, width + 128), BF16),
        vmem((width, ff), BF16), vmem((width, ff), BF16), vmem((ff, width), BF16),
        vmem((total, width), BF16), vmem((total, width), BF16), vmem((total, width), BF16),
        vmem((total, width), F32), vmem((total, 128), F32),
        vmem((total, ff), BF16), vmem((total, ff), BF16),
        vmem((total, 128), F32), vmem((total, 128), F32),
        vmem((32, width), F32), vmem((32, total), F32), vmem((32, total), F32),
        vmem((2, blocks, t, wide), BF16), vmem((2, plane, experts, t, wide), BF16),
        vmem((2, plane - 1, experts, t, wide), BF16), vmem((2, plane - 1, experts, t, wide), BF16),
        vmem((2, experts, t, wide), BF16), vmem((2, experts, t, wide), BF16),
        vmem((total, 128), F32),
        vmem((1, vec), F32), vmem((1, vec), F32), vmem((1, vec), F32), vmem((3, 1, vec), F32),
        vmem((1, vec), F32), vmem((experts, 1, vec), F32),
        dma((2,)), dma((12,)), dma((blocks, 2)), dma((steps, 2, 2)), dma((steps, 2)), dma((steps, 2)),
        dma((steps, 4, 2)), dma((steps,)), dma((steps,)),
        dma((2, 4)), dma((2, 4)), dma((2, 3)), dma((2, 3)), dma((2, experts)), dma((2, experts)),
        dma((4 + experts,)), dma((4 + experts,)),
    ]
    inside = pl.BlockSpec(memory_space=pltpu.VMEM)
    outside = pl.BlockSpec(memory_space=pl.ANY)
    results = pl.pallas_call(
        functools.partial(dense_kernel, experts),
        out_shape=(
            jax.ShapeDtypeStruct((t, width), BF16),
            jax.ShapeDtypeStruct((experts, width), F32),
            jax.ShapeDtypeStruct((1, width), F32),
        ),
        in_specs=[outside, outside, inside, outside, outside, outside, inside, inside],
        out_specs=(inside, inside, inside),
        scratch_shapes=scratch,
        compiler_params=pltpu.CompilerParams(
            collective_id=0, has_side_effects=True, vmem_limit_bytes=60 * 2**20
        ),
    )(tokens, cotangent, expert_picks.T, w_gate, w_up, w_down, router, norm_gain.reshape(1, width))
    grad, router_grad, gain_grad = pl.pallas_call(
        hand_on,
        out_shape=tuple(jax.ShapeDtypeStruct(r.shape, r.dtype) for r in results),
        in_specs=[inside] * 3,
        out_specs=(inside,) * 3,
    )(*results)
    return grad, router_grad, gain_grad.reshape(width)


def local(tokens, cotangent, expert_picks, w_gate, w_up, w_down, router, norm_gain):
    experts = lax.axis_size("expert")
    groups = lax.axis_size("dp")
    tok_count = tokens.shape[0]
    feature_width = tokens.shape[1]
    capacity = 4 * tok_count // experts
    gate_shard = w_gate[0]
    up_shard = w_up[0]
    down_shard = w_down[0]
    x_float = tokens.astype(jnp.float32)
    inverse = 1.0 / jnp.sqrt(jnp.mean(x_float * x_float, axis=-1, keepdims=True) + EPSILON)
    normed = x_float * inverse
    hidden = (normed * norm_gain).astype(jnp.bfloat16)
    hidden_float = hidden.astype(jnp.float32)
    logits = lax.dot_general(
        hidden_float, router, (((1,), (1,)), ((), ())), precision=highest_precision
    )
    expert_ids = jnp.arange(experts, dtype=jnp.int32)
    first_hot = (expert_picks[:, 0:1] == expert_ids).astype(jnp.float32)
    second_hot = (expert_picks[:, 1:2] == expert_ids).astype(jnp.float32)
    gate_first = jax.nn.sigmoid(jnp.sum(logits * first_hot, -1) - jnp.sum(logits * second_hot, -1))
    gate_second = 1.0 - gate_first
    pair_expert = expert_picks.reshape(-1)
    pair_hot = (pair_expert[:, None] == expert_ids).astype(jnp.int32)
    slot_rank = jnp.sum(jnp.cumsum(pair_hot, axis=0) * pair_hot, axis=1) - 1
    empty_slots = jnp.zeros((experts, capacity, feature_width), jnp.bfloat16)
    send_rows = empty_slots.at[pair_expert, slot_rank].set(jnp.repeat(hidden, 2, axis=0))
    send_cots = empty_slots.at[pair_expert, slot_rank].set(jnp.repeat(cotangent, 2, axis=0))
    arrived_rows, arrived_cots = (
        lax.all_to_all(send_rows, "expert", split_axis=0, concat_axis=0, tiled=True),
        lax.all_to_all(send_cots, "expert", split_axis=0, concat_axis=0, tiled=True),
    )
    group_rows, group_cots = (
        lax.all_gather(arrived_rows, "dp", axis=0, tiled=True),
        lax.all_gather(arrived_cots, "dp", axis=0, tiled=True),
    )
    d_rows, pick_part = expert_pass(
        group_rows.reshape(-1, feature_width),
        group_cots.reshape(-1, feature_width),
        gate_shard,
        up_shard,
        down_shard,
    )
    pick_grid = pick_part.reshape(groups, experts, capacity)
    summed = lax.psum_scatter(
        d_rows.reshape(groups * experts, capacity, feature_width).astype(jnp.bfloat16),
        "dp",
        scatter_dimension=0,
        tiled=True,
    )
    grad_back = lax.all_to_all(summed, "expert", split_axis=0, concat_axis=0, tiled=True)
    column_hot = (expert_ids == lax.axis_index("expert")).astype(jnp.float32)
    pick_table = pick_grid[:, :, None, :] * column_hot[None, None, :, None]
    pick_total = lax.psum(pick_table, ("dp", "expert"))
    pick_mine = pick_total[lax.axis_index("dp"), lax.axis_index("expert")]
    pick_inner = pick_mine[pair_expert, slot_rank].reshape(tok_count, 2)
    grad_pairs = (
        grad_back[pair_expert, slot_rank].astype(jnp.float32).reshape(tok_count, 2, feature_width)
    )
    gate_delta = gate_first * gate_second * (pick_inner[:, 0] - pick_inner[:, 1])
    logit_grad = (first_hot - second_hot) * gate_delta[:, None]
    hidden_grad = gate_first[:, None] * grad_pairs[:, 0] + gate_second[:, None] * grad_pairs[:, 1]
    hidden_grad = hidden_grad + jnp.dot(logit_grad, router, precision=highest_precision)
    router_part = lax.dot_general(
        logit_grad, hidden_float, (((0,), (0,)), ((), ())), precision=highest_precision
    )
    gain_part = jnp.sum(hidden_grad * normed, axis=0)
    router_grad, gain_grad = lax.psum((router_part, gain_part), ("dp", "expert"))
    scaled_grad = hidden_grad * norm_gain
    token_grad = cotangent.astype(jnp.float32) + inverse * (
        scaled_grad - normed * jnp.mean(scaled_grad * normed, axis=-1, keepdims=True)
    )
    return (token_grad.astype(jnp.bfloat16), router_grad, gain_grad)


def solution(mesh):
    in_specs = (
        P(("dp", "expert"), None),
        P(("dp", "expert"), None),
        P(("dp", "expert"), None),
        P("expert", None, "dp"),
        P("expert", None, "dp"),
        P("expert", "dp", None),
        P(),
        P(),
    )
    out_specs = (P(("dp", "expert"), None), P(), P())
    groups, experts = mesh.shape["dp"], mesh.shape["expert"]
    body = dense if experts in (2, 4) and groups == 2**3 else local
    return jax.shard_map(body, mesh=mesh, in_specs=in_specs, out_specs=out_specs, check_vma=False)
```

```python
import functools

import jax
import jax.numpy as jnp
from jax import lax
from jax.experimental import pallas as pl
from jax.experimental.pallas import tpu as pltpu
from jax.sharding import PartitionSpec as P

EPSILON = 1e-05
highest_precision = lax.Precision.HIGHEST


def silu_grad(pre_act):
    sigmoid_value = jax.nn.sigmoid(pre_act)
    return sigmoid_value + pre_act * sigmoid_value * (1.0 - sigmoid_value)


def expert_pass(slot_rows, slot_cots, gate_shard, up_shard, down_shard):
    pre_gate = jnp.dot(slot_rows, gate_shard, preferred_element_type=jnp.float32)
    pre_up = jnp.dot(slot_rows, up_shard, preferred_element_type=jnp.float32)
    act = (jax.nn.silu(pre_gate) * pre_up).astype(jnp.bfloat16)
    cot_back = lax.dot_general(
        slot_cots, down_shard, (((1,), (1,)), ((), ())), preferred_element_type=jnp.float32
    )
    pick_part = jnp.sum(act.astype(jnp.float32) * cot_back, -1)
    d_gate = (cot_back * pre_up * silu_grad(pre_gate)).astype(jnp.bfloat16)
    d_up = (cot_back * jax.nn.silu(pre_gate)).astype(jnp.bfloat16)
    d_rows = lax.dot_general(
        d_gate, gate_shard, (((1,), (1,)), ((), ())), preferred_element_type=jnp.float32
    )
    d_rows = d_rows + lax.dot_general(
        d_up, up_shard, (((1,), (1,)), ((), ())), preferred_element_type=jnp.float32
    )
    return (d_rows, pick_part)


NT = (((1,), (1,)), ((), ()))
F32 = jnp.float32
BF16 = jnp.bfloat16


def split3(v):
    hi = v.astype(BF16).astype(F32)
    mid = (v - hi).astype(BF16).astype(F32)
    return hi, mid, v - hi - mid


def store_split(ref, v):
    n = v.shape[0]
    ref[...] = jnp.zeros_like(ref)
    for i, part in enumerate(split3(v)):
        ref[8 * i : 8 * i + n, :] = part


def join_split(v, n):
    return v[0:n] + v[8 : 8 + n] + v[16 : 16 + n]


def dense_kernel(
    experts, tok_ref, cot_ref, picks_ref, wg_hbm, wu_hbm, wd_hbm, router_ref, gain_ref,
    out_tok, out_router, out_gain,
    buf, wg, wu, wd, hid, tok, cot, norm, inv, dg, du, wcol, lgcol, rsp, lsp, lspi,
    pbuf, cbuf, sbuf, plbuf, zsrc, zbuf, pickcol, vsrc, cvec, vchip, pvec, vplane, zvec,
    lsem, wsem, agr, zs, xs, ys, cs, dxs, dys, rs_s, rs_r, pl_s, pl_r, zz_s, zz_r, vs, vr,
):
    width = tok_ref.shape[1]
    tok_count = tok_ref.shape[0]
    blocks = buf.shape[0]
    total = blocks * tok_count
    ff = wg.shape[1]
    dp = lax.axis_index("dp")
    ex = lax.axis_index("expert")
    core = lax.rem(dp, 2)
    group = lax.div(dp, 2)
    xbit = lax.rem(group, 2)
    ybit = lax.div(group, 2)
    to_core = 1 - 2 * core
    to_x = 1 - 2 * xbit
    to_y = 2 * (1 - 2 * ybit)
    dp_c = dp + to_core
    dp_x = dp + 2 * to_x
    dp_y = dp + 2 * to_y
    dp_d = dp + 2 * (to_x + to_y)
    me = dp * experts + ex

    tile = ff // 4
    wcopies = []
    for t in range(4):
        part = pl.ds(t * tile, tile)
        three = (
            pltpu.make_async_copy(wg_hbm.at[0, :, part], wg.at[:, part], wsem.at[3 * t]),
            pltpu.make_async_copy(wu_hbm.at[0, :, part], wu.at[:, part], wsem.at[3 * t + 1]),
            pltpu.make_async_copy(wd_hbm.at[0, part, :], wd.at[part, :], wsem.at[3 * t + 2]),
        )
        wcopies.append(three)
    def where_is(d, z):
        return {"dp": d, "expert": z}

    barrier = pltpu.get_barrier_semaphore()
    def greet(d, z):
        pl.semaphore_signal(barrier, inc=1, device_id=where_is(d, z), device_id_type=pl.DeviceIdType.MESH)

    for d in (dp_c, dp_x, dp_y):
        greet(d, ex)
    pl.when(ex > 0)(lambda: greet(dp, ex - 1))
    pl.when(ex + 1 < experts)(lambda: greet(dp, ex + 1))
    load_t = pltpu.make_async_copy(tok_ref, buf.at[me, 0, :, pl.ds(0, width)], lsem.at[0])
    load_c = pltpu.make_async_copy(cot_ref, buf.at[me, 1, :, pl.ds(0, width)], lsem.at[1])
    load_t.start()
    load_c.start()
    picks = picks_ref[...].astype(F32)
    lane = lax.broadcasted_iota(jnp.int32, (tok_count, 128), 1)
    diagonal = lax.broadcasted_iota(jnp.int32, (tok_count, tok_count), 0) == lax.broadcasted_iota(
        jnp.int32, (tok_count, tok_count), 1
    )
    first_pick = jnp.sum(jnp.where(diagonal, picks[0:1, :], 0.0), axis=1, keepdims=True)
    second_pick = jnp.sum(jnp.where(diagonal, picks[1:2, :], 0.0), axis=1, keepdims=True)
    picks_tile = jnp.where(lane == 0, first_pick, jnp.where(lane == 1, second_pick, 0.0))
    buf[me, 0, :, width : width + 128] = picks_tile.astype(BF16)
    buf[me, 1, :, width : width + 128] = jnp.zeros((tok_count, 128), BF16)
    pl.semaphore_wait(barrier, 3 + jnp.minimum(ex, 1) + jnp.minimum(experts - 1 - ex, 1))
    load_t.wait()
    load_c.wait()

    def rcopy(src, dst, ssem, rsem, d, z):
        return pltpu.make_async_remote_copy(
            src_ref=src, dst_ref=dst, send_sem=ssem, recv_sem=rsem,
            device_id=where_is(d, z), device_id_type=pl.DeviceIdType.MESH,
        )

    pending = []

    def begin(copy, pred=None):
        if pred is None:
            copy.start()
        else:
            pl.when(pred)(copy.start)
        pending.append((copy, pred))

    def both(a, b):
        return b if a is None else (a if b is None else jnp.logical_and(a, b))

    def slot_copy(slot, ssem, d, z, half):
        view = buf.at[slot, half]
        return rcopy(view, view, ssem, agr.at[slot, half], d, z)

    order = [(0, 0)]
    for k in range(1, experts):
        order += [(k, -1), (k, 1)]

    def origin(k, side):
        z = ex + side * k
        if k == 0:
            return z, None
        return z, (z >= 0 if side < 0 else z < experts)

    def sidx(k, side):
        return 2 * k + (1 if side > 0 else 0)

    def guarded(ok, fn):
        if ok is None:
            fn()
        else:
            pl.when(ok)(fn)

    def z_step(k, side, half):
        z, ok = origin(k, side)
        slot = dp * experts + z
        i = sidx(k, side)
        if k:
            pl.when(ok)(slot_copy(slot, zs.at[i, 0, half], dp, ex, half).wait_recv)
        if side <= 0:
            begin(slot_copy(slot, zs.at[i, 0, half], dp, ex + 1, half), both(ok, ex + 1 < experts))
        if side >= 0:
            begin(slot_copy(slot, zs.at[i, 1, half], dp, ex - 1, half), both(ok, ex > 0))
        begin(slot_copy(slot, xs.at[i, half], dp_x, ex, half), ok)
        begin(slot_copy(slot, ys.at[i, half], dp_y, ex, half), ok)
        if k >= experts - 1:
            begin(slot_copy(slot, (dys, dxs)[half].at[i], dp_d, ex, half), ok)
        begin(slot_copy(slot, cs.at[i, 0, half], dp_c, ex, half), ok)

    def xy_step(k, side):
        z, ok = origin(k, side)
        i = sidx(k, side)
        from_x = dp_x * experts + z
        from_y = dp_y * experts + z
        guarded(ok, slot_copy(from_x, xs.at[i, 0], dp_x, ex, 0).wait_recv)
        if k < experts - 1:
            begin(slot_copy(from_x, dys.at[i], dp_y, ex, 0), ok)
        begin(slot_copy(from_x, cs.at[i, 1, 0], dp_c, ex, 0), ok)
        guarded(ok, slot_copy(from_y, ys.at[i, 1], dp_y, ex, 1).wait_recv)
        if k < experts - 1:
            begin(slot_copy(from_y, dxs.at[i], dp_x, ex, 1), ok)
        begin(slot_copy(from_y, cs.at[i, 2, 1], dp_c, ex, 1), ok)
        guarded(ok, slot_copy(from_x, xs.at[i, 1], dp_x, ex, 1).wait_recv)
        begin(slot_copy(from_x, cs.at[i, 1, 1], dp_c, ex, 1), ok)
        guarded(ok, slot_copy(from_y, ys.at[i, 0], dp_y, ex, 0).wait_recv)
        begin(slot_copy(from_y, cs.at[i, 2, 0], dp_c, ex, 0), ok)

    def diag_step(k, side):
        z, ok = origin(k, side)
        i = sidx(k, side)
        slot = dp_d * experts + z
        guarded(ok, slot_copy(slot, dys.at[i], dp_y, ex, 0).wait_recv)
        begin(slot_copy(slot, cs.at[i, 3, 0], dp_c, ex, 0), ok)
        guarded(ok, slot_copy(slot, dxs.at[i], dp_x, ex, 1).wait_recv)
        begin(slot_copy(slot, cs.at[i, 3, 1], dp_c, ex, 1), ok)

    gain = gain_ref[...]

    def prepare(j, carry):
        rows = pl.ds(pl.multiple_of(j * 2 * tok_count, 2 * tok_count), 2 * tok_count)
        x = buf[pl.ds(2 * j, 2), 0, :, 0:width].astype(F32).reshape(2 * tok_count, width)
        inverse = 1.0 / jnp.sqrt(jnp.mean(x * x, axis=-1, keepdims=True) + EPSILON)
        normed = x * inverse
        norm[rows, :] = normed
        inv[rows, :] = jnp.broadcast_to(inverse, (2 * tok_count, 128))
        tok[rows, :] = x.astype(BF16)
        hid[rows, :] = (normed * gain).astype(BF16)
        c = buf[pl.ds(2 * j, 2), 1, :, 0:width].astype(F32).reshape(2 * tok_count, width)
        cot[rows, :] = c.astype(BF16)
        wcol[rows, :] = buf[pl.ds(2 * j, 2), 0, :, width : width + 128].astype(F32).reshape(2 * tok_count, 128)
        return carry

    def prepare_rows(d):
        pairs = experts // 2
        lax.fori_loop(0, pairs, lambda i, carry: prepare(d * pairs + i, carry), 0)

    for k in range(experts + 2):
        for half in range(2):
            for kk, side in order:
                if kk == k:
                    z_step(kk, side, half)
        if k == 0:
            for three in wcopies:
                for cp in three:
                    cp.start()
        for kk, side in order:
            if kk == k - 1:
                xy_step(kk, side)
        for kk, side in order:
            if kk == k - 2:
                diag_step(kk, side)
        if k == experts:
            for d in (dp, dp_x, dp_y):
                prepare_rows(d)
    prepare_rows(dp_d)
    for d in (dp_c, dp_x + to_core, dp_y + to_core, dp_d + to_core):
        for z in range(experts):
            for half in range(2):
                slot_copy(d * experts + z, cs.at[0, 0, 0], dp_c, ex, half).wait_recv()
        prepare_rows(d)


    router = router_ref[...]
    store_split(rsp, router)
    logits = join_split(
        lax.dot_general(rsp[...].astype(BF16), hid[...], NT, preferred_element_type=F32), experts
    )
    pick_rows = wcol[...].T
    first, second = pick_rows[0:1, :], pick_rows[1:2, :]
    ids = lax.broadcasted_iota(jnp.int32, (experts, total), 0).astype(F32)
    first_hot = (first == ids).astype(F32)
    second_hot = (second == ids).astype(F32)
    gate_first = jax.nn.sigmoid(
        jnp.sum(logits * first_hot, 0, keepdims=True) - jnp.sum(logits * second_hot, 0, keepdims=True)
    )
    gate_second = 1.0 - gate_first
    here = ex.astype(F32)
    mine_first = (first == here).astype(F32)
    mine_second = (second == here).astype(F32)
    weight = gate_first * mine_first + gate_second * mine_second
    wcol[...] = jnp.broadcast_to(weight, (128, total)).T

    pick = jnp.zeros((total, 1), F32)
    for t in range(4):
        for cp in wcopies[t]:
            cp.wait()
        a, b = t * tile, (t + 1) * tile
        pre_gate = jnp.dot(hid[...], wg[:, a:b], preferred_element_type=F32)
        pre_up = jnp.dot(hid[...], wu[:, a:b], preferred_element_type=F32)
        back = lax.dot_general(cot[...], wd[a:b, :], NT, preferred_element_type=F32)
        s = jax.nn.sigmoid(pre_gate)
        silu = pre_gate * s
        act = (silu * pre_up).astype(BF16).astype(F32)
        pick = pick + jnp.sum(act * back, -1, keepdims=True)
        dg[:, a:b] = (back * pre_up * (s + silu * (1.0 - s))).astype(BF16)
        du[:, a:b] = (back * silu).astype(BF16)
    pick_row = jnp.broadcast_to(pick, (total, 128)).T[0:1, :]
    vsrc[:, width : width + total] = pick_row * (mine_first - mine_second)

    chunks = pbuf.shape[0]
    wide = width // chunks
    step = wide // 2

    def backward(c, h):
        a = c * wide + h * step
        part = lax.dot_general(dg[...], wg[a : a + step, :], NT, preferred_element_type=F32)
        part = part + lax.dot_general(du[...], wu[a : a + step, :], NT, preferred_element_type=F32)
        part = part * jnp.concatenate([wcol[...]] * (step // 128), axis=1)
        vsrc[:, a : a + step] = jnp.sum(part * norm[:, a : a + step], axis=0, keepdims=True)
        pbuf[c, :, :, h * step : (h + 1) * step] = part.reshape(blocks, tok_count, step).astype(BF16)

    g_of = [group + to_x + to_y, group + to_x, group + to_y, group]
    halves = {}
    planes = {}

    def core_stage(c):
        for i, g in enumerate(g_of):
            src = pbuf.at[c, pl.ds((2 * g + 1 - core) * experts, experts)]
            halves[c, i] = rcopy(src, cbuf.at[c, i], rs_s.at[c, i], rs_r.at[c, i], dp_c, ex)
            begin(halves[c, i])

    def plane_stage(c):
        for i, d in enumerate((dp_d, dp_x, dp_y)):
            halves[c, i].wait_recv()
            own = pbuf[c, pl.ds((2 * g_of[i] + core) * experts, experts)].astype(F32)
            sbuf[c, i] = (own + cbuf[c, i].astype(F32)).astype(BF16)
            planes[c, i] = rcopy(sbuf.at[c, i], plbuf.at[c, i], pl_s.at[c, i], pl_r.at[c, i], d, ex)
            begin(planes[c, i])

    own_base = (2 * group + core) * experts

    def plane_sum(c, z):
        v = pbuf[c, own_base + z].astype(F32) + cbuf[c, 3, z].astype(F32)
        for i in range(3):
            v = v + plbuf[c, i, z].astype(F32)
        return v

    def z_stage(c):
        halves[c, 3].wait_recv()
        for i in range(3):
            planes[c, i].wait_recv()
        for k in range(1, experts):
            z = lax.rem(ex + k, experts)
            zsrc[c, z] = plane_sum(c, z).astype(BF16)
            begin(rcopy(zsrc.at[c, z], zbuf.at[c, ex], zz_s.at[c, k], zz_r.at[c, ex], dp, z))
        return plane_sum(c, ex)

    backward(0, 0)
    backward(0, 1)
    core_stage(0)
    backward(1, 0)
    plane_stage(0)
    backward(1, 1)
    core_stage(1)
    vcore = rcopy(vsrc, cvec, vs.at[0], vr.at[0], dp_c, ex)
    begin(vcore)
    plane_stage(1)
    vcore.wait_recv()
    vchip[...] = vsrc[...] + cvec[...]
    vplanes = []
    for j, dd in enumerate((dp_d, dp_x, dp_y)):
        vp = rcopy(vchip, pvec.at[j], vs.at[1 + j], vr.at[1 + j], dd, ex)
        begin(vp)
        vplanes.append(vp)
    sums = [z_stage(0)]
    for vp in vplanes:
        vp.wait_recv()
    vplane[...] = (vchip[...] + pvec[1]) + (pvec[2] + pvec[0])
    zvec[ex] = vplane[...]
    for k in range(1, experts):
        z = lax.rem(ex + k, experts)
        begin(rcopy(vplane, zvec.at[ex], vs.at[4 + k], vr.at[4 + ex], dp, z))
    sums.append(z_stage(1))
    hidden_grad = jnp.concatenate(sums, axis=1)

    for k in range(1, experts):
        z = lax.rem(ex + k, experts)
        rcopy(vplane, zvec.at[z], vs.at[4 + k], vr.at[4 + z], dp, z).wait_recv()
    vec = zvec[0]
    for z in range(1, experts):
        vec = vec + zvec[z]
    gate_delta = gate_first * gate_second * vec[:, width : width + total]
    logit_grad = (first_hot - second_hot) * gate_delta
    store_split(lsp, logit_grad)
    inv_row = inv[...].T[0:1, :]
    store_split(lspi, logit_grad * inv_row)
    out_router[...] = join_split(jnp.dot(lsp[...].astype(BF16), hid[...], preferred_element_type=F32), experts)
    by_norm = join_split(jnp.dot(lspi[...].astype(BF16), tok[...], preferred_element_type=F32), experts)
    out_gain[...] = vec[:, 0:width] + jnp.sum(by_norm * router, axis=0, keepdims=True)
    lanes = lax.broadcasted_iota(jnp.int32, (128, total), 0)
    spread = jnp.zeros((128, total), F32)
    for e in range(experts):
        spread = jnp.where(lanes == e, logit_grad[e : e + 1, :], spread)
    lgcol[...] = spread.T
    rows = pl.ds(pl.multiple_of(me * tok_count, tok_count), tok_count)
    mine = lgcol[rows, :]
    for e in range(experts):
        hidden_grad = hidden_grad + mine[:, e : e + 1] * router[e : e + 1, :]
    for k in range(1, experts):
        z = lax.rem(ex + k, experts)
        arrived = []
        for c in range(chunks):
            rcopy(zsrc.at[c, z], zbuf.at[c, z], zz_s.at[c, k], zz_r.at[c, z], dp, z).wait_recv()
            arrived.append(zbuf[c, z].astype(F32))
        hidden_grad = hidden_grad + jnp.concatenate(arrived, axis=1)
    scaled = hidden_grad * gain
    normed = norm[rows, :]
    grad = buf[me, 1, :, 0:width].astype(F32) + inv[rows, 0:1] * (
        scaled - normed * jnp.mean(scaled * normed, axis=-1, keepdims=True)
    )
    out_tok[...] = grad.astype(BF16)
    for cp, pred in pending:
        guarded(pred, cp.wait_send)


def hand_on(a_in, b_in, c_in, a_out, b_out, c_out):
    a_out[...] = a_in[...]
    b_out[...] = b_in[...]
    c_out[...] = c_in[...]


def dense(tokens, cotangent, expert_picks, w_gate, w_up, w_down, router, norm_gain):
    experts = lax.axis_size("expert")
    groups = lax.axis_size("dp")
    t, width = tokens.shape
    ff = w_gate.shape[2]
    blocks = experts * groups
    total = blocks * t
    plane = groups // 2
    steps = 2 * experts
    vec = width + total
    wide = width // 2
    dma = pltpu.SemaphoreType.DMA
    vmem = pltpu.VMEM
    scratch = [
        vmem((blocks, 2, t, width + 128), BF16),
        vmem((width, ff), BF16), vmem((width, ff), BF16), vmem((ff, width), BF16),
        vmem((total, width), BF16), vmem((total, width), BF16), vmem((total, width), BF16),
        vmem((total, width), F32), vmem((total, 128), F32),
        vmem((total, ff), BF16), vmem((total, ff), BF16),
        vmem((total, 128), F32), vmem((total, 128), F32),
        vmem((32, width), F32), vmem((32, total), F32), vmem((32, total), F32),
        vmem((2, blocks, t, wide), BF16), vmem((2, plane, experts, t, wide), BF16),
        vmem((2, plane - 1, experts, t, wide), BF16), vmem((2, plane - 1, experts, t, wide), BF16),
        vmem((2, experts, t, wide), BF16), vmem((2, experts, t, wide), BF16),
        vmem((total, 128), F32),
        vmem((1, vec), F32), vmem((1, vec), F32), vmem((1, vec), F32), vmem((3, 1, vec), F32),
        vmem((1, vec), F32), vmem((experts, 1, vec), F32),
        dma((2,)), dma((12,)), dma((blocks, 2)), dma((steps, 2, 2)), dma((steps, 2)), dma((steps, 2)),
        dma((steps, 4, 2)), dma((steps,)), dma((steps,)),
        dma((2, 4)), dma((2, 4)), dma((2, 3)), dma((2, 3)), dma((2, experts)), dma((2, experts)),
        dma((4 + experts,)), dma((4 + experts,)),
    ]
    inside = pl.BlockSpec(memory_space=pltpu.VMEM)
    outside = pl.BlockSpec(memory_space=pl.ANY)
    results = pl.pallas_call(
        functools.partial(dense_kernel, experts),
        out_shape=(
            jax.ShapeDtypeStruct((t, width), BF16),
            jax.ShapeDtypeStruct((experts, width), F32),
            jax.ShapeDtypeStruct((1, width), F32),
        ),
        in_specs=[outside, outside, inside, outside, outside, outside, inside, inside],
        out_specs=(inside, inside, inside),
        scratch_shapes=scratch,
        compiler_params=pltpu.CompilerParams(
            collective_id=0, has_side_effects=True, vmem_limit_bytes=60 * 2**20
        ),
    )(tokens, cotangent, expert_picks.T, w_gate, w_up, w_down, router, norm_gain.reshape(1, width))
    grad, router_grad, gain_grad = pl.pallas_call(
        hand_on,
        out_shape=tuple(jax.ShapeDtypeStruct(r.shape, r.dtype) for r in results),
        in_specs=[inside] * 3,
        out_specs=(inside,) * 3,
    )(*results)
    return grad, router_grad, gain_grad.reshape(width)


def local(tokens, cotangent, expert_picks, w_gate, w_up, w_down, router, norm_gain):
    experts = lax.axis_size("expert")
    groups = lax.axis_size("dp")
    tok_count = tokens.shape[0]
    feature_width = tokens.shape[1]
    capacity = 4 * tok_count // experts
    gate_shard = w_gate[0]
    up_shard = w_up[0]
    down_shard = w_down[0]
    x_float = tokens.astype(jnp.float32)
    inverse = 1.0 / jnp.sqrt(jnp.mean(x_float * x_float, axis=-1, keepdims=True) + EPSILON)
    normed = x_float * inverse
    hidden = (normed * norm_gain).astype(jnp.bfloat16)
    hidden_float = hidden.astype(jnp.float32)
    logits = lax.dot_general(
        hidden_float, router, (((1,), (1,)), ((), ())), precision=highest_precision
    )
    expert_ids = jnp.arange(experts, dtype=jnp.int32)
    first_hot = (expert_picks[:, 0:1] == expert_ids).astype(jnp.float32)
    second_hot = (expert_picks[:, 1:2] == expert_ids).astype(jnp.float32)
    gate_first = jax.nn.sigmoid(jnp.sum(logits * first_hot, -1) - jnp.sum(logits * second_hot, -1))
    gate_second = 1.0 - gate_first
    pair_expert = expert_picks.reshape(-1)
    pair_hot = (pair_expert[:, None] == expert_ids).astype(jnp.int32)
    slot_rank = jnp.sum(jnp.cumsum(pair_hot, axis=0) * pair_hot, axis=1) - 1
    empty_slots = jnp.zeros((experts, capacity, feature_width), jnp.bfloat16)
    send_rows = empty_slots.at[pair_expert, slot_rank].set(jnp.repeat(hidden, 2, axis=0))
    send_cots = empty_slots.at[pair_expert, slot_rank].set(jnp.repeat(cotangent, 2, axis=0))
    arrived_rows, arrived_cots = (
        lax.all_to_all(send_rows, "expert", split_axis=0, concat_axis=0, tiled=True),
        lax.all_to_all(send_cots, "expert", split_axis=0, concat_axis=0, tiled=True),
    )
    group_rows, group_cots = (
        lax.all_gather(arrived_rows, "dp", axis=0, tiled=True),
        lax.all_gather(arrived_cots, "dp", axis=0, tiled=True),
    )
    d_rows, pick_part = expert_pass(
        group_rows.reshape(-1, feature_width),
        group_cots.reshape(-1, feature_width),
        gate_shard,
        up_shard,
        down_shard,
    )
    pick_grid = pick_part.reshape(groups, experts, capacity)
    summed = lax.psum_scatter(
        d_rows.reshape(groups * experts, capacity, feature_width).astype(jnp.bfloat16),
        "dp",
        scatter_dimension=0,
        tiled=True,
    )
    grad_back = lax.all_to_all(summed, "expert", split_axis=0, concat_axis=0, tiled=True)
    column_hot = (expert_ids == lax.axis_index("expert")).astype(jnp.float32)
    pick_table = pick_grid[:, :, None, :] * column_hot[None, None, :, None]
    pick_total = lax.psum(pick_table, ("dp", "expert"))
    pick_mine = pick_total[lax.axis_index("dp"), lax.axis_index("expert")]
    pick_inner = pick_mine[pair_expert, slot_rank].reshape(tok_count, 2)
    grad_pairs = (
        grad_back[pair_expert, slot_rank].astype(jnp.float32).reshape(tok_count, 2, feature_width)
    )
    gate_delta = gate_first * gate_second * (pick_inner[:, 0] - pick_inner[:, 1])
    logit_grad = (first_hot - second_hot) * gate_delta[:, None]
    hidden_grad = gate_first[:, None] * grad_pairs[:, 0] + gate_second[:, None] * grad_pairs[:, 1]
    hidden_grad = hidden_grad + jnp.dot(logit_grad, router, precision=highest_precision)
    router_part = lax.dot_general(
        logit_grad, hidden_float, (((0,), (0,)), ((), ())), precision=highest_precision
    )
    gain_part = jnp.sum(hidden_grad * normed, axis=0)
    router_grad, gain_grad = lax.psum((router_part, gain_part), ("dp", "expert"))
    scaled_grad = hidden_grad * norm_gain
    token_grad = cotangent.astype(jnp.float32) + inverse * (
        scaled_grad - normed * jnp.mean(scaled_grad * normed, axis=-1, keepdims=True)
    )
    return (token_grad.astype(jnp.bfloat16), router_grad, gain_grad)


def solution(mesh):
    in_specs = (
        P(("dp", "expert"), None),
        P(("dp", "expert"), None),
        P(("dp", "expert"), None),
        P("expert", None, "dp"),
        P("expert", None, "dp"),
        P("expert", "dp", None),
        P(),
        P(),
    )
    out_specs = (P(("dp", "expert"), None), P(), P())
    groups, experts = mesh.shape["dp"], mesh.shape["expert"]
    body = dense if experts in (2, 4) and groups == 2**3 else local
    return jax.shard_map(body, mesh=mesh, in_specs=in_specs, out_specs=out_specs, check_vma=False)
```

```python
import functools

import jax
import jax.numpy as jnp
from jax import lax
from jax.experimental import pallas as pl
from jax.experimental.pallas import tpu as pltpu
from jax.sharding import PartitionSpec as P

EPSILON = 1e-05
highest_precision = lax.Precision.HIGHEST


def silu_grad(pre_act):
    sigmoid_value = jax.nn.sigmoid(pre_act)
    return sigmoid_value + pre_act * sigmoid_value * (1.0 - sigmoid_value)


def expert_pass(slot_rows, slot_cots, gate_shard, up_shard, down_shard):
    pre_gate = jnp.dot(slot_rows, gate_shard, preferred_element_type=jnp.float32)
    pre_up = jnp.dot(slot_rows, up_shard, preferred_element_type=jnp.float32)
    act = (jax.nn.silu(pre_gate) * pre_up).astype(jnp.bfloat16)
    cot_back = lax.dot_general(
        slot_cots, down_shard, (((1,), (1,)), ((), ())), preferred_element_type=jnp.float32
    )
    pick_part = jnp.sum(act.astype(jnp.float32) * cot_back, -1)
    d_gate = (cot_back * pre_up * silu_grad(pre_gate)).astype(jnp.bfloat16)
    d_up = (cot_back * jax.nn.silu(pre_gate)).astype(jnp.bfloat16)
    d_rows = lax.dot_general(
        d_gate, gate_shard, (((1,), (1,)), ((), ())), preferred_element_type=jnp.float32
    )
    d_rows = d_rows + lax.dot_general(
        d_up, up_shard, (((1,), (1,)), ((), ())), preferred_element_type=jnp.float32
    )
    return (d_rows, pick_part)


NT = (((1,), (1,)), ((), ()))
F32 = jnp.float32
BF16 = jnp.bfloat16


def split3(v):
    hi = v.astype(BF16).astype(F32)
    mid = (v - hi).astype(BF16).astype(F32)
    return hi, mid, v - hi - mid


def store_split(ref, v):
    n = v.shape[0]
    ref[...] = jnp.zeros_like(ref)
    for i, part in enumerate(split3(v)):
        ref[8 * i : 8 * i + n, :] = part


def join_split(v, n):
    return v[0:n] + v[8 : 8 + n] + v[16 : 16 + n]


def dense_kernel(
    experts, tok_ref, cot_ref, picks_ref, wg_hbm, wu_hbm, wd_hbm, router_ref, gain_ref,
    out_tok, out_router, out_gain,
    buf, wg, wu, wd, hid, tok, cot, norm, inv, dg, du, wcol, lgcol, rsp, lsp, lspi,
    pbuf, cbuf, sbuf, plbuf, zsrc, zbuf, pickcol, vsrc, cvec, vchip, pvec, vplane, zvec,
    lsem, wsem, agr, zs, xs, ys, cs, dxs, dys, rs_s, rs_r, pl_s, pl_r, zz_s, zz_r, vs, vr,
):
    width = tok_ref.shape[1]
    tok_count = tok_ref.shape[0]
    blocks = buf.shape[0]
    total = blocks * tok_count
    ff = wg.shape[1]
    dp = lax.axis_index("dp")
    ex = lax.axis_index("expert")
    core = lax.rem(dp, 2)
    group = lax.div(dp, 2)
    xbit = lax.rem(group, 2)
    ybit = lax.div(group, 2)
    to_core = 1 - 2 * core
    to_x = 1 - 2 * xbit
    to_y = 2 * (1 - 2 * ybit)
    dp_c = dp + to_core
    dp_x = dp + 2 * to_x
    dp_y = dp + 2 * to_y
    dp_d = dp + 2 * (to_x + to_y)
    me = dp * experts + ex

    tile = ff // 4
    wcopies = []
    for t in range(4):
        part = pl.ds(t * tile, tile)
        three = (
            pltpu.make_async_copy(wg_hbm.at[0, :, part], wg.at[:, part], wsem.at[3 * t]),
            pltpu.make_async_copy(wu_hbm.at[0, :, part], wu.at[:, part], wsem.at[3 * t + 1]),
            pltpu.make_async_copy(wd_hbm.at[0, part, :], wd.at[part, :], wsem.at[3 * t + 2]),
        )
        wcopies.append(three)
    def where_is(d, z):
        return {"dp": d, "expert": z}

    barrier = pltpu.get_barrier_semaphore()
    def greet(d, z):
        pl.semaphore_signal(barrier, inc=1, device_id=where_is(d, z), device_id_type=pl.DeviceIdType.MESH)

    for d in (dp_c, dp_x, dp_y):
        greet(d, ex)
    pl.when(ex > 0)(lambda: greet(dp, ex - 1))
    pl.when(ex + 1 < experts)(lambda: greet(dp, ex + 1))
    load_t = pltpu.make_async_copy(tok_ref, buf.at[me, 0, :, pl.ds(0, width)], lsem.at[0])
    load_c = pltpu.make_async_copy(cot_ref, buf.at[me, 1, :, pl.ds(0, width)], lsem.at[1])
    load_t.start()
    load_c.start()
    picks = picks_ref[...].astype(F32)
    lane = lax.broadcasted_iota(jnp.int32, (tok_count, 128), 1)
    diagonal = lax.broadcasted_iota(jnp.int32, (tok_count, tok_count), 0) == lax.broadcasted_iota(
        jnp.int32, (tok_count, tok_count), 1
    )
    first_pick = jnp.sum(jnp.where(diagonal, picks[0:1, :], 0.0), axis=1, keepdims=True)
    second_pick = jnp.sum(jnp.where(diagonal, picks[1:2, :], 0.0), axis=1, keepdims=True)
    picks_tile = jnp.where(lane == 0, first_pick, jnp.where(lane == 1, second_pick, 0.0))
    buf[me, 0, :, width : width + 128] = picks_tile.astype(BF16)
    buf[me, 1, :, width : width + 128] = jnp.zeros((tok_count, 128), BF16)
    pl.semaphore_wait(barrier, 3 + jnp.minimum(ex, 1) + jnp.minimum(experts - 1 - ex, 1))
    load_t.wait()
    load_c.wait()

    def rcopy(src, dst, ssem, rsem, d, z):
        return pltpu.make_async_remote_copy(
            src_ref=src, dst_ref=dst, send_sem=ssem, recv_sem=rsem,
            device_id=where_is(d, z), device_id_type=pl.DeviceIdType.MESH,
        )

    pending = []

    def begin(copy, pred=None):
        if pred is None:
            copy.start()
        else:
            pl.when(pred)(copy.start)
        pending.append((copy, pred))

    def both(a, b):
        return b if a is None else (a if b is None else jnp.logical_and(a, b))

    def slot_copy(slot, ssem, d, z, half):
        view = buf.at[slot, half]
        return rcopy(view, view, ssem, agr.at[slot, half], d, z)

    order = [(0, 0)]
    for k in range(1, experts):
        order += [(k, -1), (k, 1)]

    def origin(k, side):
        z = ex + side * k
        if k == 0:
            return z, None
        return z, (z >= 0 if side < 0 else z < experts)

    def sidx(k, side):
        return 2 * k + (1 if side > 0 else 0)

    def guarded(ok, fn):
        if ok is None:
            fn()
        else:
            pl.when(ok)(fn)

    def z_step(k, side, half):
        z, ok = origin(k, side)
        slot = dp * experts + z
        i = sidx(k, side)
        if k:
            pl.when(ok)(slot_copy(slot, zs.at[i, 0, half], dp, ex, half).wait_recv)
        if side <= 0:
            begin(slot_copy(slot, zs.at[i, 0, half], dp, ex + 1, half), both(ok, ex + 1 < experts))
        if side >= 0:
            begin(slot_copy(slot, zs.at[i, 1, half], dp, ex - 1, half), both(ok, ex > 0))
        begin(slot_copy(slot, xs.at[i, half], dp_x, ex, half), ok)
        begin(slot_copy(slot, ys.at[i, half], dp_y, ex, half), ok)
        if k >= experts - 1:
            begin(slot_copy(slot, (dys, dxs)[half].at[i], dp_d, ex, half), ok)
        begin(slot_copy(slot, cs.at[i, 0, half], dp_c, ex, half), ok)

    def xy_step(k, side):
        z, ok = origin(k, side)
        i = sidx(k, side)
        from_x = dp_x * experts + z
        from_y = dp_y * experts + z
        guarded(ok, slot_copy(from_x, xs.at[i, 0], dp_x, ex, 0).wait_recv)
        if k < experts - 1:
            begin(slot_copy(from_x, dys.at[i], dp_y, ex, 0), ok)
        begin(slot_copy(from_x, cs.at[i, 1, 0], dp_c, ex, 0), ok)
        guarded(ok, slot_copy(from_y, ys.at[i, 1], dp_y, ex, 1).wait_recv)
        if k < experts - 1:
            begin(slot_copy(from_y, dxs.at[i], dp_x, ex, 1), ok)
        begin(slot_copy(from_y, cs.at[i, 2, 1], dp_c, ex, 1), ok)
        guarded(ok, slot_copy(from_x, xs.at[i, 1], dp_x, ex, 1).wait_recv)
        begin(slot_copy(from_x, cs.at[i, 1, 1], dp_c, ex, 1), ok)
        guarded(ok, slot_copy(from_y, ys.at[i, 0], dp_y, ex, 0).wait_recv)
        begin(slot_copy(from_y, cs.at[i, 2, 0], dp_c, ex, 0), ok)

    def diag_step(k, side):
        z, ok = origin(k, side)
        i = sidx(k, side)
        slot = dp_d * experts + z
        guarded(ok, slot_copy(slot, dys.at[i], dp_y, ex, 0).wait_recv)
        begin(slot_copy(slot, cs.at[i, 3, 0], dp_c, ex, 0), ok)
        guarded(ok, slot_copy(slot, dxs.at[i], dp_x, ex, 1).wait_recv)
        begin(slot_copy(slot, cs.at[i, 3, 1], dp_c, ex, 1), ok)

    gain = gain_ref[...]

    def prepare(j, carry):
        rows = pl.ds(pl.multiple_of(j * 2 * tok_count, 2 * tok_count), 2 * tok_count)
        x = buf[pl.ds(2 * j, 2), 0, :, 0:width].astype(F32).reshape(2 * tok_count, width)
        inverse = 1.0 / jnp.sqrt(jnp.mean(x * x, axis=-1, keepdims=True) + EPSILON)
        normed = x * inverse
        norm[rows, :] = normed
        inv[rows, :] = jnp.broadcast_to(inverse, (2 * tok_count, 128))
        tok[rows, :] = x.astype(BF16)
        hid[rows, :] = (normed * gain).astype(BF16)
        c = buf[pl.ds(2 * j, 2), 1, :, 0:width].astype(F32).reshape(2 * tok_count, width)
        cot[rows, :] = c.astype(BF16)
        wcol[rows, :] = buf[pl.ds(2 * j, 2), 0, :, width : width + 128].astype(F32).reshape(2 * tok_count, 128)
        return carry

    def prepare_rows(d):
        pairs = experts // 2
        lax.fori_loop(0, pairs, lambda i, carry: prepare(d * pairs + i, carry), 0)

    for k in range(experts + 2):
        for half in range(2):
            for kk, side in order:
                if kk == k:
                    z_step(kk, side, half)
        if k == 1:
            for three in wcopies:
                for cp in three:
                    cp.start()
        for kk, side in order:
            if kk == k - 1:
                xy_step(kk, side)
        for kk, side in order:
            if kk == k - 2:
                diag_step(kk, side)
        if k == experts:
            for d in (dp, dp_x, dp_y):
                prepare_rows(d)
    prepare_rows(dp_d)
    for d in (dp_c, dp_x + to_core, dp_y + to_core, dp_d + to_core):
        for z in range(experts):
            for half in range(2):
                slot_copy(d * experts + z, cs.at[0, 0, 0], dp_c, ex, half).wait_recv()
        prepare_rows(d)


    router = router_ref[...]
    store_split(rsp, router)
    logits = join_split(
        lax.dot_general(rsp[...].astype(BF16), hid[...], NT, preferred_element_type=F32), experts
    )
    pick_rows = wcol[...].T
    first, second = pick_rows[0:1, :], pick_rows[1:2, :]
    ids = lax.broadcasted_iota(jnp.int32, (experts, total), 0).astype(F32)
    first_hot = (first == ids).astype(F32)
    second_hot = (second == ids).astype(F32)
    gate_first = jax.nn.sigmoid(
        jnp.sum(logits * first_hot, 0, keepdims=True) - jnp.sum(logits * second_hot, 0, keepdims=True)
    )
    gate_second = 1.0 - gate_first
    here = ex.astype(F32)
    mine_first = (first == here).astype(F32)
    mine_second = (second == here).astype(F32)
    weight = gate_first * mine_first + gate_second * mine_second
    wcol[...] = jnp.broadcast_to(weight, (128, total)).T

    pick = jnp.zeros((total, 1), F32)
    for t in range(4):
        for cp in wcopies[t]:
            cp.wait()
        a, b = t * tile, (t + 1) * tile
        pre_gate = jnp.dot(hid[...], wg[:, a:b], preferred_element_type=F32)
        pre_up = jnp.dot(hid[...], wu[:, a:b], preferred_element_type=F32)
        back = lax.dot_general(cot[...], wd[a:b, :], NT, preferred_element_type=F32)
        s = jax.nn.sigmoid(pre_gate)
        silu = pre_gate * s
        act = (silu * pre_up).astype(BF16).astype(F32)
        pick = pick + jnp.sum(act * back, -1, keepdims=True)
        dg[:, a:b] = (back * pre_up * (s + silu * (1.0 - s))).astype(BF16)
        du[:, a:b] = (back * silu).astype(BF16)
    pick_row = jnp.broadcast_to(pick, (total, 128)).T[0:1, :]
    vsrc[:, width : width + total] = pick_row * (mine_first - mine_second)

    chunks = pbuf.shape[0]
    wide = width // chunks
    step = wide // 2

    def backward(c, h):
        a = c * wide + h * step
        part = lax.dot_general(dg[...], wg[a : a + step, :], NT, preferred_element_type=F32)
        part = part + lax.dot_general(du[...], wu[a : a + step, :], NT, preferred_element_type=F32)
        part = part * jnp.concatenate([wcol[...]] * (step // 128), axis=1)
        vsrc[:, a : a + step] = jnp.sum(part * norm[:, a : a + step], axis=0, keepdims=True)
        pbuf[c, :, :, h * step : (h + 1) * step] = part.reshape(blocks, tok_count, step).astype(BF16)

    g_of = [group + to_x + to_y, group + to_x, group + to_y, group]
    halves = {}
    planes = {}

    def core_stage(c):
        for i, g in enumerate(g_of):
            src = pbuf.at[c, pl.ds((2 * g + 1 - core) * experts, experts)]
            halves[c, i] = rcopy(src, cbuf.at[c, i], rs_s.at[c, i], rs_r.at[c, i], dp_c, ex)
            begin(halves[c, i])

    def plane_stage(c):
        for i, d in enumerate((dp_d, dp_x, dp_y)):
            halves[c, i].wait_recv()
            own = pbuf[c, pl.ds((2 * g_of[i] + core) * experts, experts)].astype(F32)
            sbuf[c, i] = (own + cbuf[c, i].astype(F32)).astype(BF16)
            planes[c, i] = rcopy(sbuf.at[c, i], plbuf.at[c, i], pl_s.at[c, i], pl_r.at[c, i], d, ex)
            begin(planes[c, i])

    own_base = (2 * group + core) * experts

    def plane_sum(c, z):
        v = pbuf[c, own_base + z].astype(F32) + cbuf[c, 3, z].astype(F32)
        for i in range(3):
            v = v + plbuf[c, i, z].astype(F32)
        return v

    def z_stage(c):
        halves[c, 3].wait_recv()
        for i in range(3):
            planes[c, i].wait_recv()
        for k in range(1, experts):
            z = lax.rem(ex + k, experts)
            zsrc[c, z] = plane_sum(c, z).astype(BF16)
            begin(rcopy(zsrc.at[c, z], zbuf.at[c, ex], zz_s.at[c, k], zz_r.at[c, ex], dp, z))
        return plane_sum(c, ex)

    backward(0, 0)
    backward(0, 1)
    core_stage(0)
    backward(1, 0)
    plane_stage(0)
    backward(1, 1)
    core_stage(1)
    vcore = rcopy(vsrc, cvec, vs.at[0], vr.at[0], dp_c, ex)
    begin(vcore)
    plane_stage(1)
    vcore.wait_recv()
    vchip[...] = vsrc[...] + cvec[...]
    vplanes = []
    for j, dd in enumerate((dp_d, dp_x, dp_y)):
        vp = rcopy(vchip, pvec.at[j], vs.at[1 + j], vr.at[1 + j], dd, ex)
        begin(vp)
        vplanes.append(vp)
    sums = [z_stage(0)]
    for vp in vplanes:
        vp.wait_recv()
    vplane[...] = (vchip[...] + pvec[1]) + (pvec[2] + pvec[0])
    zvec[ex] = vplane[...]
    for k in range(1, experts):
        z = lax.rem(ex + k, experts)
        begin(rcopy(vplane, zvec.at[ex], vs.at[4 + k], vr.at[4 + ex], dp, z))
    sums.append(z_stage(1))
    hidden_grad = jnp.concatenate(sums, axis=1)

    for k in range(1, experts):
        z = lax.rem(ex + k, experts)
        rcopy(vplane, zvec.at[z], vs.at[4 + k], vr.at[4 + z], dp, z).wait_recv()
    vec = zvec[0]
    for z in range(1, experts):
        vec = vec + zvec[z]
    gate_delta = gate_first * gate_second * vec[:, width : width + total]
    logit_grad = (first_hot - second_hot) * gate_delta
    store_split(lsp, logit_grad)
    inv_row = inv[...].T[0:1, :]
    store_split(lspi, logit_grad * inv_row)
    out_router[...] = join_split(jnp.dot(lsp[...].astype(BF16), hid[...], preferred_element_type=F32), experts)
    by_norm = join_split(jnp.dot(lspi[...].astype(BF16), tok[...], preferred_element_type=F32), experts)
    out_gain[...] = vec[:, 0:width] + jnp.sum(by_norm * router, axis=0, keepdims=True)
    lanes = lax.broadcasted_iota(jnp.int32, (128, total), 0)
    spread = jnp.zeros((128, total), F32)
    for e in range(experts):
        spread = jnp.where(lanes == e, logit_grad[e : e + 1, :], spread)
    lgcol[...] = spread.T
    rows = pl.ds(pl.multiple_of(me * tok_count, tok_count), tok_count)
    mine = lgcol[rows, :]
    for e in range(experts):
        hidden_grad = hidden_grad + mine[:, e : e + 1] * router[e : e + 1, :]
    for k in range(1, experts):
        z = lax.rem(ex + k, experts)
        arrived = []
        for c in range(chunks):
            rcopy(zsrc.at[c, z], zbuf.at[c, z], zz_s.at[c, k], zz_r.at[c, z], dp, z).wait_recv()
            arrived.append(zbuf[c, z].astype(F32))
        hidden_grad = hidden_grad + jnp.concatenate(arrived, axis=1)
    scaled = hidden_grad * gain
    normed = norm[rows, :]
    grad = buf[me, 1, :, 0:width].astype(F32) + inv[rows, 0:1] * (
        scaled - normed * jnp.mean(scaled * normed, axis=-1, keepdims=True)
    )
    out_tok[...] = grad.astype(BF16)
    for cp, pred in pending:
        guarded(pred, cp.wait_send)


def hand_on(a_in, b_in, c_in, a_out, b_out, c_out):
    a_out[...] = a_in[...]
    b_out[...] = b_in[...]
    c_out[...] = c_in[...]


def dense(tokens, cotangent, expert_picks, w_gate, w_up, w_down, router, norm_gain):
    experts = lax.axis_size("expert")
    groups = lax.axis_size("dp")
    t, width = tokens.shape
    ff = w_gate.shape[2]
    blocks = experts * groups
    total = blocks * t
    plane = groups // 2
    steps = 2 * experts
    vec = width + total
    wide = width // 2
    dma = pltpu.SemaphoreType.DMA
    vmem = pltpu.VMEM
    scratch = [
        vmem((blocks, 2, t, width + 128), BF16),
        vmem((width, ff), BF16), vmem((width, ff), BF16), vmem((ff, width), BF16),
        vmem((total, width), BF16), vmem((total, width), BF16), vmem((total, width), BF16),
        vmem((total, width), F32), vmem((total, 128), F32),
        vmem((total, ff), BF16), vmem((total, ff), BF16),
        vmem((total, 128), F32), vmem((total, 128), F32),
        vmem((32, width), F32), vmem((32, total), F32), vmem((32, total), F32),
        vmem((2, blocks, t, wide), BF16), vmem((2, plane, experts, t, wide), BF16),
        vmem((2, plane - 1, experts, t, wide), BF16), vmem((2, plane - 1, experts, t, wide), BF16),
        vmem((2, experts, t, wide), BF16), vmem((2, experts, t, wide), BF16),
        vmem((total, 128), F32),
        vmem((1, vec), F32), vmem((1, vec), F32), vmem((1, vec), F32), vmem((3, 1, vec), F32),
        vmem((1, vec), F32), vmem((experts, 1, vec), F32),
        dma((2,)), dma((12,)), dma((blocks, 2)), dma((steps, 2, 2)), dma((steps, 2)), dma((steps, 2)),
        dma((steps, 4, 2)), dma((steps,)), dma((steps,)),
        dma((2, 4)), dma((2, 4)), dma((2, 3)), dma((2, 3)), dma((2, experts)), dma((2, experts)),
        dma((4 + experts,)), dma((4 + experts,)),
    ]
    inside = pl.BlockSpec(memory_space=pltpu.VMEM)
    outside = pl.BlockSpec(memory_space=pl.ANY)
    results = pl.pallas_call(
        functools.partial(dense_kernel, experts),
        out_shape=(
            jax.ShapeDtypeStruct((t, width), BF16),
            jax.ShapeDtypeStruct((experts, width), F32),
            jax.ShapeDtypeStruct((1, width), F32),
        ),
        in_specs=[outside, outside, inside, outside, outside, outside, inside, inside],
        out_specs=(inside, inside, inside),
        scratch_shapes=scratch,
        compiler_params=pltpu.CompilerParams(
            collective_id=0, has_side_effects=True, vmem_limit_bytes=60 * 2**20
        ),
    )(tokens, cotangent, expert_picks.T, w_gate, w_up, w_down, router, norm_gain.reshape(1, width))
    grad, router_grad, gain_grad = pl.pallas_call(
        hand_on,
        out_shape=tuple(jax.ShapeDtypeStruct(r.shape, r.dtype) for r in results),
        in_specs=[inside] * 3,
        out_specs=(inside,) * 3,
    )(*results)
    return grad, router_grad, gain_grad.reshape(width)


def local(tokens, cotangent, expert_picks, w_gate, w_up, w_down, router, norm_gain):
    experts = lax.axis_size("expert")
    groups = lax.axis_size("dp")
    tok_count = tokens.shape[0]
    feature_width = tokens.shape[1]
    capacity = 4 * tok_count // experts
    gate_shard = w_gate[0]
    up_shard = w_up[0]
    down_shard = w_down[0]
    x_float = tokens.astype(jnp.float32)
    inverse = 1.0 / jnp.sqrt(jnp.mean(x_float * x_float, axis=-1, keepdims=True) + EPSILON)
    normed = x_float * inverse
    hidden = (normed * norm_gain).astype(jnp.bfloat16)
    hidden_float = hidden.astype(jnp.float32)
    logits = lax.dot_general(
        hidden_float, router, (((1,), (1,)), ((), ())), precision=highest_precision
    )
    expert_ids = jnp.arange(experts, dtype=jnp.int32)
    first_hot = (expert_picks[:, 0:1] == expert_ids).astype(jnp.float32)
    second_hot = (expert_picks[:, 1:2] == expert_ids).astype(jnp.float32)
    gate_first = jax.nn.sigmoid(jnp.sum(logits * first_hot, -1) - jnp.sum(logits * second_hot, -1))
    gate_second = 1.0 - gate_first
    pair_expert = expert_picks.reshape(-1)
    pair_hot = (pair_expert[:, None] == expert_ids).astype(jnp.int32)
    slot_rank = jnp.sum(jnp.cumsum(pair_hot, axis=0) * pair_hot, axis=1) - 1
    empty_slots = jnp.zeros((experts, capacity, feature_width), jnp.bfloat16)
    send_rows = empty_slots.at[pair_expert, slot_rank].set(jnp.repeat(hidden, 2, axis=0))
    send_cots = empty_slots.at[pair_expert, slot_rank].set(jnp.repeat(cotangent, 2, axis=0))
    arrived_rows, arrived_cots = (
        lax.all_to_all(send_rows, "expert", split_axis=0, concat_axis=0, tiled=True),
        lax.all_to_all(send_cots, "expert", split_axis=0, concat_axis=0, tiled=True),
    )
    group_rows, group_cots = (
        lax.all_gather(arrived_rows, "dp", axis=0, tiled=True),
        lax.all_gather(arrived_cots, "dp", axis=0, tiled=True),
    )
    d_rows, pick_part = expert_pass(
        group_rows.reshape(-1, feature_width),
        group_cots.reshape(-1, feature_width),
        gate_shard,
        up_shard,
        down_shard,
    )
    pick_grid = pick_part.reshape(groups, experts, capacity)
    summed = lax.psum_scatter(
        d_rows.reshape(groups * experts, capacity, feature_width).astype(jnp.bfloat16),
        "dp",
        scatter_dimension=0,
        tiled=True,
    )
    grad_back = lax.all_to_all(summed, "expert", split_axis=0, concat_axis=0, tiled=True)
    column_hot = (expert_ids == lax.axis_index("expert")).astype(jnp.float32)
    pick_table = pick_grid[:, :, None, :] * column_hot[None, None, :, None]
    pick_total = lax.psum(pick_table, ("dp", "expert"))
    pick_mine = pick_total[lax.axis_index("dp"), lax.axis_index("expert")]
    pick_inner = pick_mine[pair_expert, slot_rank].reshape(tok_count, 2)
    grad_pairs = (
        grad_back[pair_expert, slot_rank].astype(jnp.float32).reshape(tok_count, 2, feature_width)
    )
    gate_delta = gate_first * gate_second * (pick_inner[:, 0] - pick_inner[:, 1])
    logit_grad = (first_hot - second_hot) * gate_delta[:, None]
    hidden_grad = gate_first[:, None] * grad_pairs[:, 0] + gate_second[:, None] * grad_pairs[:, 1]
    hidden_grad = hidden_grad + jnp.dot(logit_grad, router, precision=highest_precision)
    router_part = lax.dot_general(
        logit_grad, hidden_float, (((0,), (0,)), ((), ())), precision=highest_precision
    )
    gain_part = jnp.sum(hidden_grad * normed, axis=0)
    router_grad, gain_grad = lax.psum((router_part, gain_part), ("dp", "expert"))
    scaled_grad = hidden_grad * norm_gain
    token_grad = cotangent.astype(jnp.float32) + inverse * (
        scaled_grad - normed * jnp.mean(scaled_grad * normed, axis=-1, keepdims=True)
    )
    return (token_grad.astype(jnp.bfloat16), router_grad, gain_grad)


def solution(mesh):
    in_specs = (
        P(("dp", "expert"), None),
        P(("dp", "expert"), None),
        P(("dp", "expert"), None),
        P("expert", None, "dp"),
        P("expert", None, "dp"),
        P("expert", "dp", None),
        P(),
        P(),
    )
    out_specs = (P(("dp", "expert"), None), P(), P())
    groups, experts = mesh.shape["dp"], mesh.shape["expert"]
    body = dense if experts in (2, 4) and groups == 2**3 else local
    return jax.shard_map(body, mesh=mesh, in_specs=in_specs, out_specs=out_specs, check_vma=False)
```
